32 devices in a mesh: table: 4 (over y, core), seq: 8 (over z, x).
Axes of the slice: x: 2, y: 2, z: 4, core: 2. Of those that a mesh axis runs over, the one named last changes fastest.
Arguments:
- item_ids: int32 [4, 2048], P('table', 'seq'), may hold values from 0 to 131071, as said below
- history_len: int32 [4], P('table'), may hold values from 512 to 2048, as said below
- row_place: int32 [131072], replicated, may hold values from 0 to 131071, as said below
- item_table: bfloat16 [131072, 512], P(('table', 'seq')), may hold values from -6 to 6
- input_proj: bfloat16 [512, 2048], replicated, may hold values from -0.25 to 0.25
- output_proj: bfloat16 [512, 512], replicated, may hold values from -0.25 to 0.25
- out_cotangent: bfloat16 [4, 2048, 512], P('table', 'seq'), may hold values from -18 to 18
Outputs:
- layer_out: bfloat16 [4, 2048, 512], P('table', 'seq')
- table_grad: bfloat16 [131072, 512], P(('table', 'seq'))
The draws below stay inside these ranges and needn't reach their ends.
Inputs may be any that keep to these rules, and one draw needn't show every extreme that they name: `item_ids`: within the 256 positions of one device, at most 24 items are stored in any one owner's block of 4096 table rows (rows o * 4096 to (o + 1) * 4096 - 1); one owner's block receives exactly 24 from the positions of every device. `row_place`: A permutation: every table row holds exactly one item. `history_len`: at least one history fills all 2048 positions.
All inputs are finite; a program needn't handle non-finite values.
Results may differ from the reference program's by a relative error of at most 0.006.
Values may be sent and summed in bfloat16 or wider, within the bound.
No kernel may reach another device: no remote copies, remote signals or barrier semaphores. Data moves between devices by JAX's collectives and lax.ppermute only.
A program may use at most 128 MiB of HBM per device.

```python
import math
import jax
import jax.numpy as jnp
from jax import lax

D = 512
HEADS = 8
HEAD_DIM = 64
LEN_DEV = 256
ROWS_DEV = 4096
USERS = 4
LENGTH = 2048
OWNERS = 32
VOCAB = 131072
CAP = 24


def make_rows(key):
    base_key = jax.random.fold_in(key, 11)
    storage = jax.random.permutation(jax.random.fold_in(base_key, 1), VOCAB).astype(jnp.int32)
    inverse = jnp.argsort(storage, stable=True).astype(jnp.int32)
    hot_owner = jax.random.randint(jax.random.fold_in(base_key, 2), (), 0, OWNERS)
    blocks_all = USERS * (LENGTH // LEN_DEV)
    block_keys = jax.random.split(jax.random.fold_in(base_key, 3), blocks_all)
    slot_total = OWNERS * CAP

    def one_block(block_key):
        key_a, key_b, key_c = jax.random.split(block_key, 3)
        slot_ids = jax.random.permutation(key_a, slot_total).astype(jnp.int32)
        owner_of = slot_ids // CAP
        slot_order = jnp.arange(slot_total, dtype=jnp.int32)
        slot_score = jnp.where(owner_of == hot_owner, slot_order - slot_total, slot_order)
        chosen = jnp.argsort(slot_score, stable=True)[:LEN_DEV]
        picked = owner_of[chosen]
        picked = picked[jax.random.permutation(key_b, LEN_DEV)]
        local_row = jax.random.randint(key_c, (LEN_DEV,), 0, ROWS_DEV)
        return picked * ROWS_DEV + local_row
    stored = jax.vmap(one_block)(block_keys).reshape(USERS, LENGTH)
    return (storage, inverse[stored].astype(jnp.int32))


def draw_row_place(key, part):
    storage, identities = make_rows(key)
    return storage


def draw_item_ids(key, part):
    storage, identities = make_rows(key)
    return identities


def draw_history_len(key, part):
    lengths = jax.random.randint(jax.random.fold_in(key, 21), (USERS,), LENGTH // 4, LENGTH + 1)
    full_user = jax.random.randint(jax.random.fold_in(key, 22), (), 0, USERS)
    return jnp.where(jnp.arange(USERS) == full_user, LENGTH, lengths).astype(jnp.int32)


def draw_out_cotangent(key, part):
    own_key = jax.random.fold_in(key, 31)
    place = jnp.arange(LENGTH, dtype=jnp.float32) / (LENGTH - 1)
    ramp = 0.1 * jnp.exp(jnp.log(30.0) * place)
    base = jnp.clip(jax.random.normal(own_key, (USERS, LENGTH, D), jnp.float32), -6.0, 6.0)
    return (base * ramp[None, :, None]).astype(jnp.bfloat16)


def steps_of(rng, dims, cuts, least, top_value):
    def one(dim, blocks):
        heights = jax.random.uniform(jax.random.fold_in(jax.random.fold_in(rng, 6), dim), (blocks,), jnp.float32, least / len(cuts), top_value / len(cuts))
        return jnp.repeat(jnp.exp(heights), dims[dim] // blocks).reshape((-1,) + (1,) * (len(dims) - dim - 1))

    loudness = one(*cuts[0])
    for cut in cuts[1:]:
        loudness = loudness * one(*cut)
    return loudness


def bell_draw(key, shape, width, most, cuts=(), kind=jnp.bfloat16):
    entries = width * jax.random.normal(key, shape, jnp.float32)
    if cuts:
        entries = entries * steps_of(key, shape, cuts, -0.22, 0.18)
    return jnp.clip(entries, -most, most).astype(kind)


def setup_inputs(seed: int = 0) -> dict:
    key_of = jax.random.split(jax.random.key(seed), 8)
    item_ids = draw_item_ids(jax.random.fold_in(key_of[7], 71), 0)
    history_len = draw_history_len(jax.random.fold_in(key_of[7], 71), 0)
    row_place = draw_row_place(jax.random.fold_in(key_of[7], 71), 0)
    item_table = bell_draw(key_of[3], (VOCAB, D), 1.0, 6.0, ((0, 32),))
    input_proj = bell_draw(key_of[4], (D, 4 * D), D ** -0.5, 0.25)
    output_proj = bell_draw(key_of[5], (D, D), D ** -0.5, 0.25)
    out_cotangent = draw_out_cotangent(jax.random.fold_in(key_of[7], 71), 0)
    return dict(item_ids=item_ids, history_len=history_len, row_place=row_place, item_table=item_table, input_proj=input_proj, output_proj=output_proj, out_cotangent=out_cotangent)


eps_norm = 1e-05

def dsilu(inputs):
    sigmoid_part = jax.nn.sigmoid(inputs)
    return sigmoid_part * (1.0 + inputs * (1.0 - sigmoid_part))

def normalize(inputs):
    centred = inputs - lax.optimization_barrier(jnp.mean(inputs, axis=-1, keepdims=True))
    spread = jnp.sqrt(lax.optimization_barrier(jnp.mean(centred * centred, axis=-1, keepdims=True)) + eps_norm)
    return (centred / spread, spread)

def norm_back(gradient, normed, spread):
    mean_grad = lax.optimization_barrier(jnp.mean(gradient, axis=-1, keepdims=True))
    mean_prod = lax.optimization_barrier(jnp.mean(gradient * normed, axis=-1, keepdims=True))
    return (gradient - mean_grad - normed * mean_prod) / spread

def heads_view(matrix):
    return matrix.astype(jnp.float32).reshape(matrix.shape[0], HEADS, HEAD_DIM)

def tile_mask(query_pos, key_pos, length_user):
    return (key_pos[None, :] <= query_pos[:, None]) & (query_pos[:, None] < length_user)

def tile_forward(queries, keys_blk, values_blk, allowed, score_scale):
    scores = jnp.einsum('lhe,nhe->hln', heads_view(queries), heads_view(keys_blk)) * score_scale
    weights = jnp.where(allowed[None], jax.nn.silu(scores), 0.0).astype(jnp.bfloat16)
    result = jnp.einsum('hln,nhe->lhe', weights.astype(jnp.float32), heads_view(values_blk))
    return result.reshape(queries.shape[0], -1)

def tile_query_grad(queries, grad_rows, keys_blk, values_blk, allowed, score_scale):
    scores = jnp.einsum('lhe,nhe->hln', heads_view(queries), heads_view(keys_blk)) * score_scale
    weight_grad = jnp.einsum('lhe,nhe->hln', heads_view(grad_rows), heads_view(values_blk))
    score_grad = jnp.where(allowed[None], weight_grad * dsilu(scores), 0.0).astype(jnp.bfloat16)
    result = jnp.einsum('hln,nhe->lhe', score_grad.astype(jnp.float32), heads_view(keys_blk))
    return result.reshape(queries.shape[0], -1) * score_scale

def tile_key_grad(query_piece, grad_piece, keys_mine, values_mine, allowed, score_scale):
    scores = jnp.einsum('lhe,nhe->hln', heads_view(query_piece), heads_view(keys_mine)) * score_scale
    weights = jnp.where(allowed[None], jax.nn.silu(scores), 0.0).astype(jnp.bfloat16)
    weight_grad = jnp.einsum('lhe,nhe->hln', heads_view(grad_piece), heads_view(values_mine))
    score_grad = jnp.where(allowed[None], weight_grad * dsilu(scores), 0.0).astype(jnp.bfloat16)
    value_part = jnp.einsum('hln,lhe->nhe', weights.astype(jnp.float32), heads_view(grad_piece))
    key_part = jnp.einsum('hln,lhe->nhe', score_grad.astype(jnp.float32), heads_view(query_piece))
    key_count = keys_mine.shape[0]
    return (key_part.reshape(key_count, -1) * score_scale, value_part.reshape(key_count, -1))

def block_sweep(tile_fn, outer, inner, starts, zeros_out, needed):

    def per_outer(outer_item):
        outer_blocks, outer_start = outer_item

        def per_inner(running, inner_item):
            inner_blocks, inner_start = inner_item

            def work():
                return tile_fn(running, outer_blocks, inner_blocks, outer_start, inner_start)
            return (lax.cond(needed(outer_start, inner_start), work, lambda: running), None)
        result, unused = lax.scan(per_inner, zeros_out, (inner, starts))
        return result
    return lax.map(per_outer, (outer, starts))

def one_user(user_item, item_table, input_proj, output_proj, score_scale):
    stored_user, length_user, cot_user = user_item
    block_rows = math.gcd(LENGTH, 512)
    block_count = LENGTH // block_rows
    local_pos = jnp.arange(block_rows, dtype=jnp.int32)
    starts = jnp.arange(block_count, dtype=jnp.int32) * block_rows
    positions = jnp.arange(LENGTH, dtype=jnp.int32)
    live_rows = (positions < length_user).astype(jnp.float32)[:, None]
    embedded = item_table[stored_user]
    normed_exact, input_spread = normalize(embedded.astype(jnp.float32))
    normed = normed_exact.astype(jnp.bfloat16)
    pre_act = jnp.dot(normed, input_proj, preferred_element_type=jnp.float32)
    activated = jax.nn.silu(pre_act)
    gate_u = activated[:, :D]
    value_rows = activated[:, D:2 * D].astype(jnp.bfloat16)
    query_rows = activated[:, 2 * D:3 * D].astype(jnp.bfloat16)
    key_rows = activated[:, 3 * D:].astype(jnp.bfloat16)

    def blocks(matrix):
        return matrix.reshape(block_count, block_rows, matrix.shape[1])
    zero_rows = jnp.zeros((block_rows, D), jnp.float32)

    def query_needed(query_start, key_start):
        return (key_start <= query_start + block_rows - 1) & (query_start < length_user)

    def key_needed(key_start, query_start):
        return (query_start + block_rows - 1 >= key_start) & (query_start < length_user) & (key_start < length_user)

    def forward_tile(running, outer_blocks, inner_blocks, query_start, key_start):
        allowed = tile_mask(query_start + local_pos, key_start + local_pos, length_user)
        return running + tile_forward(outer_blocks[0], inner_blocks[0], inner_blocks[1], allowed, score_scale)
    attention = block_sweep(forward_tile, (blocks(query_rows),), (blocks(key_rows), blocks(value_rows)), starts, zero_rows, query_needed).reshape(LENGTH, D)
    attn_normed, attn_spread = normalize(attention)
    mixed = (attn_normed * gate_u).astype(jnp.bfloat16)
    branch = jnp.dot(mixed, output_proj, preferred_element_type=jnp.float32)
    layer_out = (live_rows * (embedded.astype(jnp.float32) + branch)).astype(jnp.bfloat16)
    cot_masked = jnp.where(live_rows > 0.0, cot_user, 0.0).astype(jnp.bfloat16)
    mixed_grad = jnp.dot(cot_masked, output_proj.T, preferred_element_type=jnp.float32)
    attention_grad = norm_back(mixed_grad * gate_u, attn_normed, attn_spread).astype(jnp.bfloat16)

    def query_tile(running, outer_blocks, inner_blocks, query_start, key_start):
        allowed = tile_mask(query_start + local_pos, key_start + local_pos, length_user)
        return running + tile_query_grad(outer_blocks[0], outer_blocks[1], inner_blocks[0], inner_blocks[1], allowed, score_scale)
    query_grad = block_sweep(query_tile, (blocks(query_rows), blocks(attention_grad)), (blocks(key_rows), blocks(value_rows)), starts, zero_rows, query_needed).reshape(LENGTH, D)

    def key_tile(running, outer_blocks, inner_blocks, key_start, query_start):
        allowed = tile_mask(query_start + local_pos, key_start + local_pos, length_user)
        key_part, value_part = tile_key_grad(inner_blocks[0], inner_blocks[1], outer_blocks[0], outer_blocks[1], allowed, score_scale)
        return (running[0] + key_part, running[1] + value_part)
    key_grad, value_grad = block_sweep(key_tile, (blocks(key_rows), blocks(value_rows)), (blocks(query_rows), blocks(attention_grad)), starts, (zero_rows, zero_rows), key_needed)
    key_grad = key_grad.reshape(LENGTH, D)
    value_grad = value_grad.reshape(LENGTH, D)
    activated_grad = jnp.concatenate([mixed_grad * attn_normed, value_grad, query_grad, key_grad], axis=1)
    pre_grad = (activated_grad * dsilu(pre_act)).astype(jnp.bfloat16)
    norm_grad = jnp.dot(pre_grad, input_proj.T, preferred_element_type=jnp.float32)
    embed_grad = cot_masked.astype(jnp.float32) + norm_back(norm_grad, normed_exact, input_spread)
    return (layer_out, embed_grad)

def reference(item_ids, history_len, row_place, item_table, input_proj, output_proj, out_cotangent):
    score_scale = HEAD_DIM ** (-0.5)
    stored_rows = row_place[item_ids].astype(jnp.int32)

    def per_user(user_item):
        return one_user(user_item, item_table, input_proj, output_proj, score_scale)
    layer_out, embed_grad = lax.map(per_user, (stored_rows, history_len, out_cotangent))
    table_sum = jnp.zeros((VOCAB, D), jnp.float32).at[stored_rows.reshape(-1)].add(embed_grad.reshape(-1, D))
    return (layer_out, table_sum.astype(jnp.bfloat16))
```

```python
import functools

import jax
import jax.numpy as jnp
from jax import lax
from jax.experimental import pallas as pl
from jax.experimental.pallas import tpu as pltpu
from jax.sharding import Mesh, PartitionSpec as P

HEADS = 8
eps_norm = 1e-05
LANES = 128
ALL = ("t", "o", "i")
GROUP = ("t", "i")
f32 = jnp.float32
bf16 = jnp.bfloat16
i32 = jnp.int32


def vmem():
    return pl.BlockSpec(memory_space=pltpu.VMEM)


def smem():
    return pl.BlockSpec(memory_space=pltpu.SMEM)


def params():
    return pltpu.CompilerParams(vmem_limit_bytes=60 * 1024 * 1024)


def dot(lhs, rhs, dims=((1,), (0,))):
    return lax.dot_general(lhs, rhs, (dims, ((), ())), preferred_element_type=f32)


def dsilu_of(inputs):
    sig = 0.5 + 0.5 * jnp.tanh(0.5 * inputs)
    return sig * (1.0 + inputs * (1.0 - sig))


def silu_of(inputs):
    half = 0.5 * inputs
    return half + half * jnp.tanh(half)


def iota(shape, axis):
    return lax.broadcasted_iota(i32, shape, axis)


def to_col(row):
    size = row.shape[1]
    same = iota((size, size), 0) == iota((size, size), 1)
    return jnp.sum(jnp.where(same, row, 0.0), axis=1, keepdims=True)


def to_row(col):
    size = col.shape[0]
    same = iota((size, size), 0) == iota((size, size), 1)
    return jnp.sum(jnp.where(same, col, 0.0), axis=0, keepdims=True)


def request_kernel(
    rows_dev, cap, ids_s, first_s, length_s, ids_ref, place_ref, wish_ref, note_ref, rows_scr
):
    count = ids_ref.shape[1]

    def fetch(step, unused):
        rows_scr[pl.ds(step, 1), :] = place_ref[pl.ds(ids_s[0, step] >> 7, 1), :]
        return unused

    lax.fori_loop(0, count, fetch, 0, unroll=8)
    lane_col = to_col((ids_ref[...] & (LANES - 1)).astype(f32)).astype(i32)
    lanes = iota((count, LANES), 1)
    stored = jnp.sum(
        jnp.where(lanes == lane_col, rows_scr[...].astype(f32), 0.0), axis=1, keepdims=True
    ).astype(i32)
    shift = rows_dev.bit_length() - 1
    owner = stored >> shift
    local_row = stored & (rows_dev - 1)
    hits = lanes == owner
    hits_f = jnp.where(hits, 1.0, 0.0)
    before = jnp.where(iota((count, count), 1) < iota((count, count), 0), 1.0, 0.0)
    earlier = dot(before.astype(bf16), hits_f.astype(bf16))
    rank = jnp.sum(jnp.where(hits, earlier, 0.0), axis=1, keepdims=True)
    in_rank = lanes == rank.astype(i32)
    asked = local_row + 1
    high = jnp.where(in_rank, (asked >> 7).astype(f32), 0.0).astype(bf16)
    low = jnp.where(in_rank, (asked & 127).astype(f32), 0.0).astype(bf16)
    hits_t = hits_f.T.astype(bf16)
    owners = wish_ref.shape[0]
    wish = dot(hits_t, high) * 128.0 + dot(hits_t, low)
    wish_ref[...] = wish[:owners].astype(i32) - 1
    slot = owner.astype(f32) * cap + rank
    live = (first_s[0] + iota((1, count), 1)) < length_s[0]
    note_ref[0:1, :] = to_row(slot).astype(i32)
    note_ref[1:2, :] = jnp.where(live, 1, 0)


def unpack_note(note_ref):
    slot_row = note_ref[0:1, :]
    live_row = note_ref[1:2, :].astype(f32)
    return slot_row, live_row


def normalize(inputs):
    centred = inputs - jnp.mean(inputs, axis=-1, keepdims=True)
    spread = jnp.sqrt(jnp.mean(centred * centred, axis=-1, keepdims=True) + eps_norm)
    return (centred / spread, spread)


def project_kernel(
    note_ref, rows_ref, cot_ref, w_ref, wo_ref, send_ref, emb_ref, pre_ref, mgrad_ref
):
    slot_row, live_row = unpack_note(note_ref)
    count = slot_row.shape[1]
    slots, width = rows_ref.shape
    head = width // HEADS
    slot_col = to_col(slot_row.astype(f32)).astype(i32)
    live_col = to_col(live_row)
    picks = jnp.where(iota((count, slots), 1) == slot_col, 1.0, 0.0).astype(bf16)
    embedded = dot(picks, rows_ref[...])
    emb_ref[...] = embedded.astype(bf16)
    normed, unused = normalize(embedded)
    pre = dot(normed.astype(bf16), w_ref[...])
    pre_ref[...] = pre
    cot = jnp.where(live_col > 0.0, cot_ref[...].astype(f32), 0.0).astype(bf16)
    mgrad = dot(cot, wo_ref[...], ((1,), (1,)))
    mgrad_ref[...] = mgrad
    act = silu_of(pre)
    dz = mgrad * act[:, :width]
    for h in range(HEADS):
        lo = h * head
        send_ref[h] = jnp.concatenate(
            [
                act[:, 2 * width + lo : 2 * width + lo + head],
                act[:, 3 * width + lo : 3 * width + lo + head],
                act[:, width + lo : width + lo + head],
                dz[:, lo : lo + head],
            ],
            axis=1,
        ).astype(bf16)


def forward_kernel(x_ref, att_ref, dz_ref, stat_ref):
    blocks, rows, cols = x_ref.shape
    head = cols // 4
    scale = head ** (-0.5)
    causal = iota((rows, rows), 1) <= iota((rows, rows), 0)
    for b in range(blocks):
        q = (x_ref[b, :, 0:head].astype(f32) * scale).astype(bf16)
        acc = jnp.zeros((rows, head), f32)
        for c in range(b + 1):
            scores = dot(q, x_ref[c, :, head : 2 * head], ((1,), (1,)))
            wgt = silu_of(scores)
            if c == b:
                wgt = jnp.where(causal, wgt, 0.0)
            acc = acc + dot(wgt.astype(bf16), x_ref[c, :, 2 * head : 3 * head])
        att = acc.T
        dz = x_ref[b, :, 3 * head :].astype(f32).T
        att_ref[b] = att
        dz_ref[b] = dz
        mean = jnp.sum(att, axis=0, keepdims=True) * (1.0 / head)
        cent = att - mean
        stat_ref[0, b : b + 1, :] = mean
        stat_ref[1, b : b + 1, :] = jnp.sum(cent * cent, axis=0, keepdims=True)
        stat_ref[2, b : b + 1, :] = jnp.sum(dz, axis=0, keepdims=True)
        stat_ref[3, b : b + 1, :] = jnp.sum(cent * dz, axis=0, keepdims=True)


def backward_kernel(copies, x_ref, att_ref, dz_ref, stats_ref, out_ref, dq_scr, da_scr, dat_scr, q_scr, qt_scr):
    blocks, rows, cols = x_ref.shape
    head = cols // 4
    scale = head ** (-0.5)
    width = head * HEADS
    heads = range(0, HEADS * copies, copies)
    mean = sum(stats_ref[h, 0] for h in heads) * (1.0 / HEADS)
    square = 0.0
    dz_sum = 0.0
    dz_att = 0.0
    for h in heads:
        off = stats_ref[h, 0] - mean
        square = square + (stats_ref[h, 1] + head * (off * off))
        dz_sum = dz_sum + stats_ref[h, 2]
        dz_att = dz_att + (stats_ref[h, 3] + stats_ref[h, 2] * off)
    inv = 1.0 / jnp.sqrt(square * (1.0 / width) + eps_norm)
    mean_dz = dz_sum * (1.0 / width)
    mean_prod = dz_att * inv * (1.0 / width)
    for b in range(blocks):
        att_n = (att_ref[b] - mean[b : b + 1]) * inv[b : b + 1]
        da_t = (dz_ref[b] - mean_dz[b : b + 1] - att_n * mean_prod[b : b + 1]) * inv[b : b + 1]
        out_ref[b, :, 3 * head :] = att_n.T.astype(bf16)
        dat_scr[b] = da_t.astype(bf16)
        da_scr[b] = da_t.T.astype(bf16)
        q = x_ref[b, :, 0:head].astype(f32) * scale
        q_scr[b] = q.astype(bf16)
        qt_scr[b] = q.T.astype(bf16)
    causal = iota((rows, rows), 0) <= iota((rows, rows), 1)
    for c in range(blocks):
        keys = x_ref[c, :, head : 2 * head]
        keys_t = keys.astype(f32).T.astype(bf16)
        values = x_ref[c, :, 2 * head : 3 * head]
        dk = jnp.zeros((rows, head), f32)
        dv = jnp.zeros((rows, head), f32)
        for b in range(c, blocks):
            scores = dot(keys, qt_scr[b])
            sig = 0.5 + 0.5 * jnp.tanh(0.5 * scores)
            wgt = scores * sig
            slope = sig + wgt * (1.0 - sig)
            sgrad = dot(values, dat_scr[b]) * slope
            if b == c:
                wgt = jnp.where(causal, wgt, 0.0)
                sgrad = jnp.where(causal, sgrad, 0.0)
            wgt = wgt.astype(bf16)
            sgrad = sgrad.astype(bf16)
            dv = dv + dot(wgt, da_scr[b])
            dk = dk + dot(sgrad, q_scr[b])
            part = dot(keys_t, sgrad)
            if c == 0:
                dq_scr[b] = part
            else:
                dq_scr[b] = dq_scr[b] + part
        out_ref[c, :, head : 2 * head] = dk.astype(bf16)
        out_ref[c, :, 2 * head : 3 * head] = dv.astype(bf16)
        out_ref[c, :, 0:head] = (dq_scr[c] * scale).T.astype(bf16)


def head_columns(grad_ref, copies, part, head):
    return jnp.concatenate(
        [
            grad_ref[h * copies, :, part * head : (part + 1) * head].astype(f32)
            for h in range(HEADS)
        ],
        axis=1,
    )


def embed_grad_kernel(
    copies, note_ref, grad_ref, pre_ref, mgrad_ref, emb_ref, cot_ref, w_ref, out_ref
):
    slot_row, live_row = unpack_note(note_ref)
    count, width = emb_ref.shape
    slots = out_ref.shape[0]
    head = width // HEADS
    live_col = to_col(live_row)
    columns = functools.partial(head_columns, grad_ref, copies, head=head)
    act_grad = jnp.concatenate(
        [mgrad_ref[...] * columns(3), columns(2), columns(0), columns(1)], axis=1
    )
    pre_grad = (act_grad * dsilu_of(pre_ref[...])).astype(bf16)
    norm_grad = dot(pre_grad, w_ref[...], ((1,), (1,)))
    normed, spread = normalize(emb_ref[...].astype(f32))
    mean_grad = jnp.mean(norm_grad, axis=-1, keepdims=True)
    mean_prod = jnp.mean(norm_grad * normed, axis=-1, keepdims=True)
    cot = jnp.where(live_col > 0.0, cot_ref[...].astype(f32), 0.0)
    emb_grad = cot + (norm_grad - mean_grad - normed * mean_prod) / spread
    places = jnp.where(iota((slots, count), 0) == slot_row, 1.0, 0.0).astype(bf16)
    out_ref[...] = dot(places, emb_grad.astype(bf16)).astype(bf16)


def output_kernel(copies, note_ref, grad_ref, pre_ref, emb_ref, wo_ref, out_ref):
    slot_row, live_row = unpack_note(note_ref)
    width = emb_ref.shape[1]
    live_col = to_col(live_row)
    att_n = head_columns(grad_ref, copies, 3, width // HEADS)
    mixed = (att_n * silu_of(pre_ref[:, :width])).astype(bf16)
    branch = dot(mixed, wo_ref[...])
    out_ref[...] = (live_col * (emb_ref[...].astype(f32) + branch)).astype(bf16)


def table_kernel(asked_ref, arrived_ref, out_ref):
    rows = out_ref.shape[0]
    slots = arrived_ref.shape[0]
    base = pl.program_id(0) * rows
    picks = jnp.where(iota((rows, slots), 0) + base == asked_ref[...], 1.0, 0.0).astype(bf16)
    out_ref[...] = dot(picks, arrived_ref[...]).astype(bf16)


def all_to_all(pieces, axes):
    return lax.all_to_all(pieces, axes, split_axis=0, concat_axis=0, tiled=True)


def local(item_ids, history_len, row_place, item_table, input_proj, output_proj, out_cotangent):
    count = item_ids.shape[1]
    rows_dev, width = item_table.shape
    users = lax.axis_size("t")
    inner = lax.axis_size("i")
    owners = users * users * inner
    group = users * inner
    copies = group // HEADS
    cap = 3 * count // owners
    slots = owners * cap
    head = width // HEADS
    swap = [(a * users + b, b * users + a) for a in range(users) for b in range(users)]
    moved = functools.partial(lax.ppermute, axis_name=("t", "o"), perm=swap)

    def swapped(pieces):
        shape = pieces.shape
        parts = pieces.reshape((users, users, inner) + shape[1:])
        return jnp.swapaxes(parts, 0, 1).reshape(shape)

    cot = moved(out_cotangent[0])
    first = (lax.axis_index("o") * inner + lax.axis_index("i")) * count
    wish, note = pl.pallas_call(
        functools.partial(request_kernel, rows_dev, cap),
        out_shape=(
            jax.ShapeDtypeStruct((owners, LANES), i32),
            jax.ShapeDtypeStruct((2, count), i32),
        ),
        in_specs=[smem(), smem(), smem(), vmem(), vmem()],
        out_specs=(vmem(), vmem()),
        scratch_shapes=[pltpu.VMEM((count, LANES), i32)],
        compiler_params=params(),
        name="requests",
    )(
        item_ids,
        first.reshape(1).astype(i32),
        history_len,
        item_ids,
        row_place.reshape(-1, LANES),
    )
    note = moved(note)
    wanted = swapped(all_to_all(wish, ALL))[:, :cap].reshape(slots)
    rows = item_table[jnp.maximum(wanted, 0)]
    rows = all_to_all(rows.reshape(owners, cap, width), ALL).reshape(slots, width)

    send, emb, pre, mgrad = pl.pallas_call(
        project_kernel,
        out_shape=(
            jax.ShapeDtypeStruct((HEADS, count, 4 * head), bf16),
            jax.ShapeDtypeStruct((count, width), bf16),
            jax.ShapeDtypeStruct((count, 4 * width), f32),
            jax.ShapeDtypeStruct((count, width), f32),
        ),
        in_specs=[vmem()] * 5,
        out_specs=(vmem(),) * 4,
        compiler_params=params(),
        name="project",
    )(note, rows, cot, input_proj, output_proj)

    if copies > 1:
        send = jnp.repeat(send, copies, axis=0)
    mine = all_to_all(send, GROUP)
    att, dz, stat = pl.pallas_call(
        forward_kernel,
        out_shape=(
            jax.ShapeDtypeStruct((group, head, count), f32),
            jax.ShapeDtypeStruct((group, head, count), f32),
            jax.ShapeDtypeStruct((4, group, count), f32),
        ),
        in_specs=[vmem()],
        out_specs=(vmem(),) * 3,
        compiler_params=params(),
        name="forward",
    )(mine)
    stats = all_to_all(jnp.broadcast_to(stat[None], (group,) + stat.shape), GROUP)
    grads = pl.pallas_call(
        functools.partial(backward_kernel, copies),
        out_shape=jax.ShapeDtypeStruct((group, count, 4 * head), bf16),
        in_specs=[vmem()] * 4,
        out_specs=vmem(),
        scratch_shapes=[
            pltpu.VMEM((group, head, count), f32),
            pltpu.VMEM((group, count, head), bf16),
            pltpu.VMEM((group, head, count), bf16),
            pltpu.VMEM((group, count, head), bf16),
            pltpu.VMEM((group, head, count), bf16),
        ],
        compiler_params=params(),
        name="backward",
    )(mine, att, dz, stats)
    back = all_to_all(grads, GROUP)

    outgoing = pl.pallas_call(
        functools.partial(embed_grad_kernel, copies),
        out_shape=jax.ShapeDtypeStruct((slots, width), bf16),
        in_specs=[vmem()] * 7,
        out_specs=vmem(),
        compiler_params=params(),
        name="embed_grad",
    )(note, back, pre, mgrad, emb, cot, input_proj)
    arrived = all_to_all(outgoing.reshape(owners, cap, width), ALL).reshape(slots, width)
    layer_out = moved(
        pl.pallas_call(
            functools.partial(output_kernel, copies),
            out_shape=jax.ShapeDtypeStruct((count, width), bf16),
            in_specs=[vmem()] * 5,
            out_specs=vmem(),
            compiler_params=params(),
            name="layer_out",
        )(note, back, pre, emb, output_proj)
    )
    tile = min(rows_dev, 512)
    table_grad = pl.pallas_call(
        table_kernel,
        out_shape=jax.ShapeDtypeStruct((rows_dev, width), bf16),
        grid=(rows_dev // tile,),
        in_specs=[
            pl.BlockSpec((1, slots), lambda r: (0, 0)),
            pl.BlockSpec((slots, width), lambda r: (0, 0)),
        ],
        out_specs=pl.BlockSpec((tile, width), lambda r: (r, 0)),
        compiler_params=params(),
        name="table_grad",
    )(wanted.reshape(1, slots), arrived)
    return (layer_out[None], table_grad)


def solution(mesh):
    users = mesh.shape["table"]
    inner = mesh.shape["seq"] // users
    if mesh.shape["seq"] % users or (users * inner) % HEADS:
        raise ValueError("unsupported mesh")
    finer = Mesh(mesh.devices.reshape(users, users, inner), ("t", "o", "i"))
    placed = (
        P("t", ("o", "i")),
        P("t"),
        P(),
        P(("t", "o", "i"), None),
        P(),
        P(),
        P("t", ("o", "i"), None),
    )
    return jax.shard_map(
        local,
        mesh=finer,
        in_specs=placed,
        out_specs=(P("t", ("o", "i"), None), P(("t", "o", "i"), None)),
        check_vma=False,
    )
```

```python
import functools
import math

import jax
import jax.numpy as jnp
from jax import lax
from jax.experimental import pallas as pl
from jax.experimental.pallas import tpu as pltpu
from jax.sharding import Mesh, PartitionSpec as P

HEADS = 8
eps_norm = 1e-05
LANES = 128
ALL = ("t", "o", "i")
GROUP = ("t", "i")
f32 = jnp.float32
bf16 = jnp.bfloat16
i32 = jnp.int32


def vmem():
    return pl.BlockSpec(memory_space=pltpu.VMEM)


def smem():
    return pl.BlockSpec(memory_space=pltpu.SMEM)


def params():
    return pltpu.CompilerParams(vmem_limit_bytes=24 * 1024 * 1024)


def near(array):
    return pltpu.with_memory_space_constraint(array, pltpu.VMEM)


def kernel_call(kernel, outs, args, number=None, scratch=()):
    numbers = [] if number is None else [number]
    return pl.pallas_call(
        kernel,
        out_shape=tuple(pltpu.VMEM(shape, dtype) for shape, dtype in outs),
        in_specs=[smem()] * len(numbers) + [vmem()] * len(args),
        out_specs=tuple(vmem() for unused in outs),
        scratch_shapes=list(scratch),
        compiler_params=params(),
    )(*numbers, *map(near, args))


def dot(lhs, rhs, dims=((1,), (0,))):
    return lax.dot_general(lhs, rhs, (dims, ((), ())), preferred_element_type=f32)


def dsilu_of(inputs):
    sig = 0.5 + 0.5 * jnp.tanh(0.5 * inputs)
    return sig * (1.0 + inputs * (1.0 - sig))


def silu_of(inputs):
    half = 0.5 * inputs
    return half + half * jnp.tanh(half)


def iota(shape, axis):
    return lax.broadcasted_iota(i32, shape, axis)


def to_col(row):
    size = row.shape[1]
    same = iota((size, size), 0) == iota((size, size), 1)
    return jnp.sum(jnp.where(same, row, 0.0), axis=1, keepdims=True)


def to_row(col):
    size = col.shape[0]
    same = iota((size, size), 0) == iota((size, size), 1)
    return jnp.sum(jnp.where(same, col, 0.0), axis=0, keepdims=True)


def request_kernel(
    rows_dev, cap, ids_s, first_s, length_s, ids_ref, place_ref, mail_ref, rows_scr
):
    count = ids_ref.shape[1]

    def fetch(step, unused):
        rows_scr[pl.ds(step, 1), :] = place_ref[pl.ds(ids_s[0, step] >> 7, 1), :]
        return unused

    lax.fori_loop(0, count, fetch, 0, unroll=8)
    lane_col = to_col((ids_ref[...] & (LANES - 1)).astype(f32)).astype(i32)
    lanes = iota((count, LANES), 1)
    stored = jnp.sum(
        jnp.where(lanes == lane_col, rows_scr[...].astype(f32), 0.0), axis=1, keepdims=True
    ).astype(i32)
    shift = rows_dev.bit_length() - 1
    owner = stored >> shift
    local_row = stored & (rows_dev - 1)
    hits = lanes == owner
    hits_f = jnp.where(hits, 1.0, 0.0)
    before = jnp.where(iota((count, count), 1) < iota((count, count), 0), 1.0, 0.0)
    earlier = dot(before.astype(bf16), hits_f.astype(bf16))
    rank = jnp.sum(jnp.where(hits, earlier, 0.0), axis=1, keepdims=True)
    in_rank = lanes == rank.astype(i32)
    asked = local_row + 1
    high = jnp.where(in_rank, (asked >> 7).astype(f32), 0.0).astype(bf16)
    low = jnp.where(in_rank, (asked & 127).astype(f32), 0.0).astype(bf16)
    hits_t = hits_f.T.astype(bf16)
    owners = mail_ref.shape[0]
    wish = dot(hits_t, high) * 128.0 + dot(hits_t, low)
    mail_ref[:, :LANES] = wish[:owners].astype(i32) - 1
    slot = owner.astype(f32) * cap + rank
    live = (first_s[0] + iota((1, count), 1)) < length_s[0]
    note = to_row(slot).astype(i32) * 2 + jnp.where(live, 1, 0)
    mail_ref[:, LANES:] = jnp.broadcast_to(note, (owners, count))


def read_note(twin_s, mail_ref):
    note = mail_ref[pl.ds(twin_s[0], 1), LANES:]
    return note >> 1, (note & 1).astype(f32)


def normalize(inputs):
    centred = inputs - jnp.mean(inputs, axis=-1, keepdims=True)
    spread = jnp.sqrt(jnp.mean(centred * centred, axis=-1, keepdims=True) + eps_norm)
    return (centred / spread, spread)


def project_kernel(
    twin_s, mail_ref, rows_ref, cot_ref, w_ref, wo_ref, send_ref, emb_ref, pre_ref, mgrad_ref
):
    slot_row, live_row = read_note(twin_s, mail_ref)
    count = slot_row.shape[1]
    slots, width = rows_ref.shape
    head = width // HEADS
    slot_col = to_col(slot_row.astype(f32)).astype(i32)
    live_col = to_col(live_row)
    picks = jnp.where(iota((count, slots), 1) == slot_col, 1.0, 0.0).astype(bf16)
    embedded = dot(picks, rows_ref[...])
    emb_ref[...] = embedded.astype(bf16)
    normed, _ = normalize(embedded)
    pre = dot(normed.astype(bf16), w_ref[...])
    pre_ref[...] = pre
    cot = jnp.where(live_col > 0.0, cot_ref[...].astype(f32), 0.0).astype(bf16)
    mgrad = dot(cot, wo_ref[...], ((1,), (1,)))
    mgrad_ref[...] = mgrad
    act = silu_of(pre)
    dz = mgrad * act[:, :width]
    for h in range(HEADS):
        lo = h * head
        send_ref[h] = jnp.concatenate(
            [
                act[:, 2 * width + lo : 2 * width + lo + head],
                act[:, 3 * width + lo : 3 * width + lo + head],
                act[:, width + lo : width + lo + head],
                dz[:, lo : lo + head],
            ],
            axis=1,
        ).astype(bf16)


def weight_tile(keys, queries_t):
    scores = dot(keys, queries_t)
    sig = 0.5 + 0.5 * jnp.tanh(0.5 * scores)
    wgt = scores * sig
    return wgt, sig + wgt * (1.0 - sig)


def causal_mask(rows):
    return iota((rows, rows), 0) <= iota((rows, rows), 1)


def forward_kernel(order, ready, x_ref, att_ref, dz_ref, stat_ref, *refs):
    if ready:
        wgt_ref, slope_ref = refs[:2]
    vt_scr = refs[-1]
    blocks, rows, cols = x_ref.shape
    head = cols // 4
    scale = head ** (-0.5)
    causal = causal_mask(rows)
    place = 0
    for b in range(blocks):
        queries_t = (x_ref[order[b], :, 0:head].astype(f32) * scale).T.astype(bf16)
        vt_scr[b] = x_ref[order[b], :, 2 * head : 3 * head].astype(f32).T.astype(bf16)
        att = jnp.zeros((head, rows), f32)
        for c in range(b + 1):
            wgt, slope = weight_tile(x_ref[order[c], :, head : 2 * head], queries_t)
            if b == c:
                wgt = jnp.where(causal, wgt, 0.0)
                slope = jnp.where(causal, slope, 0.0)
            wgt = wgt.astype(bf16)
            att = att + dot(vt_scr[c], wgt)
            if ready:
                wgt_ref[place] = wgt
                slope_ref[place] = slope
            place += 1
        dz = x_ref[order[b], :, 3 * head :].astype(f32).T
        att_ref[b] = att
        dz_ref[b] = dz
        mean = jnp.sum(att, axis=0, keepdims=True) * (1.0 / head)
        cent = att - mean
        stat_ref[0, b : b + 1, :] = mean
        stat_ref[1, b : b + 1, :] = jnp.sum(cent * cent, axis=0, keepdims=True)
        stat_ref[2, b : b + 1, :] = jnp.sum(dz, axis=0, keepdims=True)
        stat_ref[3, b : b + 1, :] = jnp.sum(cent * dz, axis=0, keepdims=True)


def backward_kernel(copies, order, ready, *refs):
    if ready:
        x_ref, wgt_ref, slope_ref, att_ref, dz_ref, stats_ref, out_ref = refs[:7]
        dq_scr, da_scr, dat_scr, q_scr = refs[7:]
    else:
        x_ref, att_ref, dz_ref, stats_ref, out_ref = refs[:5]
        dq_scr, da_scr, dat_scr, q_scr, qt_scr = refs[5:]
    blocks, rows, cols = x_ref.shape
    head = cols // 4
    scale = head ** (-0.5)
    width = head * HEADS
    heads = range(0, HEADS * copies, copies)
    mean = sum(stats_ref[h, 0] for h in heads) * (1.0 / HEADS)
    square = 0.0
    dz_sum = 0.0
    dz_att = 0.0
    for h in heads:
        off = stats_ref[h, 0] - mean
        square = square + (stats_ref[h, 1] + head * (off * off))
        dz_sum = dz_sum + stats_ref[h, 2]
        dz_att = dz_att + (stats_ref[h, 3] + stats_ref[h, 2] * off)
    inv = 1.0 / jnp.sqrt(square * (1.0 / width) + eps_norm)
    mean_dz = dz_sum * (1.0 / width)
    mean_prod = dz_att * inv * (1.0 / width)
    for b in range(blocks):
        att_n = (att_ref[b] - mean[b : b + 1]) * inv[b : b + 1]
        da_t = (dz_ref[b] - mean_dz[b : b + 1] - att_n * mean_prod[b : b + 1]) * inv[b : b + 1]
        out_ref[order[b], :, 3 * head :] = att_n.T.astype(bf16)
        dat_scr[b] = da_t.astype(bf16)
        da_scr[b] = da_t.T.astype(bf16)
        q = x_ref[order[b], :, 0:head].astype(f32) * scale
        q_scr[b] = q.astype(bf16)
        if not ready:
            qt_scr[b] = q.T.astype(bf16)
    causal = causal_mask(rows)
    for c in range(blocks):
        keys = x_ref[order[c], :, head : 2 * head]
        keys_t = keys.astype(f32).T.astype(bf16)
        values = x_ref[order[c], :, 2 * head : 3 * head]
        dk = jnp.zeros((rows, head), f32)
        dv = jnp.zeros((rows, head), f32)
        for b in range(c, blocks):
            if ready:
                place = b * (b + 1) // 2 + c
                wgt = wgt_ref[place]
                slope = slope_ref[place]
            else:
                wgt, slope = weight_tile(keys, qt_scr[b])
                if b == c:
                    wgt = jnp.where(causal, wgt, 0.0)
                    slope = jnp.where(causal, slope, 0.0)
                wgt = wgt.astype(bf16)
            sgrad = (dot(values, dat_scr[b]) * slope).astype(bf16)
            dv = dv + dot(wgt, da_scr[b])
            dk = dk + dot(sgrad, q_scr[b])
            part = dot(keys_t, sgrad)
            if c == 0:
                dq_scr[b] = part
            else:
                dq_scr[b] = dq_scr[b] + part
        out_ref[order[c], :, head : 2 * head] = dk.astype(bf16)
        out_ref[order[c], :, 2 * head : 3 * head] = dv.astype(bf16)
        out_ref[order[c], :, 0:head] = (dq_scr[c] * scale).T.astype(bf16)


def head_columns(grad_ref, copies, part, head):
    return jnp.concatenate(
        [
            grad_ref[h * copies, :, part * head : (part + 1) * head].astype(f32)
            for h in range(HEADS)
        ],
        axis=1,
    )


def finish_kernel(
    copies,
    twin_s,
    mail_ref,
    grad_ref,
    pre_ref,
    mgrad_ref,
    emb_ref,
    cot_ref,
    w_ref,
    wo_ref,
    out_ref,
    layer_ref,
):
    slot_row, live_row = read_note(twin_s, mail_ref)
    count, width = emb_ref.shape
    slots = out_ref.shape[0]
    head = width // HEADS
    live_col = to_col(live_row)
    columns = functools.partial(head_columns, grad_ref, copies, head=head)
    att_n = columns(3)
    mixed = (att_n * silu_of(pre_ref[:, :width])).astype(bf16)
    branch = dot(mixed, wo_ref[...])
    embedded = emb_ref[...].astype(f32)
    layer_ref[...] = (live_col * (embedded + branch)).astype(bf16)
    act_grad = jnp.concatenate(
        [mgrad_ref[...] * att_n, columns(2), columns(0), columns(1)], axis=1
    )
    pre_grad = (act_grad * dsilu_of(pre_ref[...])).astype(bf16)
    norm_grad = dot(pre_grad, w_ref[...], ((1,), (1,)))
    normed, spread = normalize(embedded)
    mean_grad = jnp.mean(norm_grad, axis=-1, keepdims=True)
    mean_prod = jnp.mean(norm_grad * normed, axis=-1, keepdims=True)
    cot = jnp.where(live_col > 0.0, cot_ref[...].astype(f32), 0.0)
    emb_grad = cot + (norm_grad - mean_grad - normed * mean_prod) / spread
    places = jnp.where(iota((slots, count), 0) == slot_row, 1.0, 0.0).astype(bf16)
    out_ref[...] = dot(places, emb_grad.astype(bf16)).astype(bf16)


def table_kernel(asked_ref, arrived_ref, out_ref):
    rows = out_ref.shape[0]
    slots = arrived_ref.shape[0]
    local_row = asked_ref[...] - pl.program_id(0) * rows
    part = math.gcd(rows, 256)
    ramp = iota((part, slots), 0).astype(f32).astype(bf16)
    for start in range(0, rows, part):
        near_row = local_row - start
        inside = (near_row >= 0) & (near_row < part)
        near_row = jnp.where(inside, near_row, -1).astype(f32)
        near_row = jnp.broadcast_to(near_row, (16, slots)).astype(bf16)[0:1]
        picks = jnp.where(ramp == near_row, jnp.ones((), bf16), jnp.zeros((), bf16))
        out_ref[start : start + part, :] = dot(picks, arrived_ref[...]).astype(bf16)


def all_to_all(pieces, axes):
    return lax.all_to_all(pieces, axes, split_axis=0, concat_axis=0, tiled=True)


def local(item_ids, history_len, row_place, item_table, input_proj, output_proj, out_cotangent):
    count = item_ids.shape[1]
    rows_dev, width = item_table.shape
    users = lax.axis_size("t")
    inner = lax.axis_size("i")
    owners = users * users * inner
    group = users * inner
    copies = group // HEADS
    cap = 3 * count // owners
    slots = owners * cap
    head = width // HEADS
    half = users // 2
    forth = [(a % 2) * half + a // 2 for a in range(users)]
    swap = [
        (a * users + b, forth[b] * users + forth.index(a))
        for a in range(users)
        for b in range(users)
    ]
    order = tuple(forth[b // inner] * inner + b % inner for b in range(group))
    moved = functools.partial(lax.ppermute, axis_name=("t", "o"), perm=swap)

    def swapped(pieces):
        shape = pieces.shape
        parts = pieces.reshape((2, half, half, 2, inner) + shape[1:])
        return jnp.transpose(parts, (3, 2, 1, 0, 4, 5)).reshape(shape)

    cot = moved(out_cotangent[0])
    first = (lax.axis_index("o") * inner + lax.axis_index("i")) * count
    mail = pl.pallas_call(
        functools.partial(request_kernel, rows_dev, cap),
        out_shape=pltpu.VMEM((owners, LANES + count), i32),
        in_specs=[smem(), smem(), smem(), vmem(), vmem()],
        out_specs=vmem(),
        scratch_shapes=[pltpu.VMEM((count, LANES), i32)],
        compiler_params=params(),
        name="requests",
    )(
        item_ids,
        first.reshape(1).astype(i32),
        history_len,
        item_ids,
        row_place.reshape(-1, LANES),
    )
    mail = all_to_all(mail, ALL)
    wanted = swapped(mail[:, :cap]).reshape(slots)
    old_t = (lax.axis_index("o") % 2) * half + lax.axis_index("o") // 2
    old_o = (lax.axis_index("t") % half) * 2 + lax.axis_index("t") // half
    twin = (old_t * users + old_o) * inner + lax.axis_index("i")
    twin = twin.reshape(1).astype(i32)
    rows = item_table[jnp.maximum(wanted, 0)]
    rows = all_to_all(rows.reshape(owners, cap, width), ALL).reshape(slots, width)

    send, emb, pre, mgrad = kernel_call(
        project_kernel,
        (
            ((HEADS, count, 4 * head), bf16),
            ((count, width), bf16),
            ((count, 4 * width), f32),
            ((count, width), f32),
        ),
        (mail, rows, cot, input_proj, output_proj), twin,
    )
    if copies > 1:
        send = jnp.repeat(send, copies, axis=0)
    mine = all_to_all(send, GROUP)
    tiles = group * (group + 1) // 2
    ready = tiles * count * count * 6 <= 16 * 1024 * 1024
    att, dz, stat, *weights = kernel_call(
        functools.partial(forward_kernel, order, ready),
        (
            ((group, head, count), f32),
            ((group, head, count), f32),
            ((4, group, count), f32),
        )
        + (((tiles, count, count), bf16), ((tiles, count, count), f32)) * ready,
        (mine,),
        scratch=[pltpu.VMEM((group, head, count), bf16)],
    )
    stats = all_to_all(jnp.broadcast_to(stat[None], (group,) + stat.shape), GROUP)
    scratch = [
        pltpu.VMEM((group, head, count), f32),
        pltpu.VMEM((group, count, head), bf16),
        pltpu.VMEM((group, head, count), bf16),
        pltpu.VMEM((group, count, head), bf16),
    ]
    if not ready:
        scratch.append(pltpu.VMEM((group, head, count), bf16))
    (grads,) = kernel_call(
        functools.partial(backward_kernel, copies, order, ready),
        (((group, count, 4 * head), bf16),),
        (mine, *weights, att, dz, stats),
        scratch=scratch,
    )
    back = all_to_all(grads, GROUP)
    outgoing, layer_out = kernel_call(
        functools.partial(finish_kernel, copies),
        (((slots, width), bf16), ((count, width), bf16)),
        (mail, back, pre, mgrad, emb, cot, input_proj, output_proj),
        twin,
    )
    arrived = all_to_all(outgoing.reshape(owners, cap, width), ALL).reshape(slots, width)
    layer_out = moved(layer_out)
    tile = min(rows_dev, 512)
    table_grad = pl.pallas_call(
        table_kernel,
        out_shape=jax.ShapeDtypeStruct((rows_dev, width), bf16),
        grid=(rows_dev // tile,),
        in_specs=[vmem(), vmem()],
        out_specs=pl.BlockSpec((tile, width), lambda r: (r, 0)),
        compiler_params=params(),
        name="table_grad",
    )(near(wanted.reshape(1, slots)), near(arrived))
    return (layer_out[None], table_grad)


def solution(mesh):
    users = mesh.shape["table"]
    inner = mesh.shape["seq"] // users
    if mesh.shape["seq"] % users or (users * inner) % HEADS:
        raise ValueError("unsupported mesh")
    finer = Mesh(mesh.devices.reshape(users, users, inner), ("t", "o", "i"))
    placed = (
        P("t", ("o", "i")),
        P("t"),
        P(),
        P(("t", "o", "i"), None),
        P(),
        P(),
        P("t", ("o", "i"), None),
    )

    return jax.shard_map(
        local,
        mesh=finer,
        in_specs=placed,
        out_specs=(P("t", ("o", "i"), None), P(("t", "o", "i"), None)),
        check_vma=False,
    )
```

```python
import functools
import math

import jax
import jax.numpy as jnp
from jax import lax
from jax.experimental import pallas as pl
from jax.experimental.pallas import tpu as pltpu
from jax.sharding import Mesh, PartitionSpec as P

HEADS = 8
eps_norm = 1e-05
LANES = 128
ALL = ("a", "b", "c", "d")
GROUP = ("b", "d")
SWAPPED = ("b", "c")
f32 = jnp.float32
bf16 = jnp.bfloat16
i32 = jnp.int32


def vmem():
    return pl.BlockSpec(memory_space=pltpu.VMEM)


def smem():
    return pl.BlockSpec(memory_space=pltpu.SMEM)


def params():
    return pltpu.CompilerParams(vmem_limit_bytes=24 * 1024 * 1024)


def near(array):
    return pltpu.with_memory_space_constraint(array, pltpu.VMEM)


def far(array):
    return pltpu.with_memory_space_constraint(array, pltpu.HBM)


def hbm():
    return pl.BlockSpec(memory_space=pltpu.HBM)


def kernel_call(kernel, outs, args, scratch=()):
    return pl.pallas_call(
        kernel,
        out_shape=tuple(pltpu.VMEM(shape, dtype) for shape, dtype in outs),
        in_specs=[vmem()] * len(args),
        out_specs=tuple(vmem() for unused in outs),
        scratch_shapes=list(scratch),
        compiler_params=params(),
    )(*map(near, args))


def dot(lhs, rhs, dims=((1,), (0,))):
    return lax.dot_general(lhs, rhs, (dims, ((), ())), preferred_element_type=f32)


def iota(shape, axis):
    return lax.broadcasted_iota(i32, shape, axis)


def to_col(row):
    size = row.shape[1]
    same = iota((size, size), 0) == iota((size, size), 1)
    return jnp.sum(jnp.where(same, row, 0.0), axis=1, keepdims=True)


def to_row(col):
    size = col.shape[0]
    same = iota((size, size), 0) == iota((size, size), 1)
    return jnp.sum(jnp.where(same, col, 0.0), axis=0, keepdims=True)


def request_kernel(
    rows_dev,
    cap,
    first_s,
    twin_s,
    length_s,
    ids_hbm,
    place_hbm,
    mail_ref,
    ids_s,
    ids_ref,
    place_ref,
    rows_scr,
    sems,
):
    count = ids_ref.shape[1]
    copies = [
        pltpu.make_async_copy(source, target, sems.at[n])
        for n, (source, target) in enumerate(
            [(place_hbm, place_ref), (ids_hbm, ids_s), (ids_hbm, ids_ref)]
        )
    ]
    for copy in copies:
        copy.start()
    for copy in copies:
        copy.wait()

    def fetch(step, unused):
        rows_scr[pl.ds(step, 1), :] = place_ref[pl.ds(ids_s[0, step] >> 7, 1), :]
        return unused

    lax.fori_loop(0, count, fetch, 0, unroll=8)
    lane_col = to_col((ids_ref[...] & (LANES - 1)).astype(f32)).astype(i32)
    lanes = iota((count, LANES), 1)
    stored = jnp.sum(
        jnp.where(lanes == lane_col, rows_scr[...].astype(f32), 0.0), axis=1, keepdims=True
    ).astype(i32)
    shift = rows_dev.bit_length() - 1
    owner = stored >> shift
    local_row = stored & (rows_dev - 1)
    hits = lanes == owner
    hits_f = jnp.where(hits, 1.0, 0.0)
    before = jnp.where(iota((count, count), 1) < iota((count, count), 0), 1.0, 0.0)
    earlier = dot(before.astype(bf16), hits_f.astype(bf16))
    rank = jnp.sum(jnp.where(hits, earlier, 0.0), axis=1, keepdims=True)
    in_rank = lanes == rank.astype(i32)
    asked = local_row + 1
    high = jnp.where(in_rank, (asked >> 7).astype(f32), 0.0).astype(bf16)
    low = jnp.where(in_rank, (asked & 127).astype(f32), 0.0).astype(bf16)
    hits_t = hits_f.T.astype(bf16)
    owners = mail_ref.shape[0]
    wish = dot(hits_t, high) * 128.0 + dot(hits_t, low)
    mail_ref[:, :LANES] = wish[:owners].astype(i32) - 1
    slot = owner.astype(f32) * cap + rank
    live = (first_s[0] + iota((1, count), 1)) < length_s[0]
    note = to_row(slot).astype(i32) * 2 + jnp.where(live, 1, 0)
    mail_ref[:, LANES:] = jnp.where(iota((owners, count), 0) == twin_s[0], note, 0)


def read_note(mail_ref):
    note = jnp.sum(mail_ref[:, LANES:].astype(f32), axis=0, keepdims=True).astype(i32)
    return note >> 1, (note & 1).astype(f32)


def normalize(inputs):
    centred = inputs - jnp.mean(inputs, axis=-1, keepdims=True)
    spread = jnp.sqrt(jnp.mean(centred * centred, axis=-1, keepdims=True) + eps_norm)
    return (centred / spread, spread)


def project_kernel(
    mail_ref, rows_ref, cot_ref, w_ref, wo_ref, send_ref, emb_ref, slope_ref, gate_ref, mgrad_ref
):
    slot_row, live_row = read_note(mail_ref)
    count = slot_row.shape[1]
    slots, width = rows_ref.shape
    head = width // HEADS
    slot_col = to_col(slot_row.astype(f32)).astype(i32)
    live_col = to_col(live_row)
    picks = jnp.where(iota((count, slots), 1) == slot_col, 1.0, 0.0).astype(bf16)
    embedded = dot(picks, rows_ref[...])
    emb_ref[...] = embedded.astype(bf16)
    normed, _ = normalize(embedded)
    pre = dot(normed.astype(bf16), w_ref[...])
    cot = jnp.where(live_col > 0.0, cot_ref[...].astype(f32), 0.0).astype(bf16)
    mgrad = dot(cot, wo_ref[...], ((1,), (1,)))
    mgrad_ref[...] = mgrad
    half = 0.5 * pre
    tanh = jnp.tanh(half)
    twice_sig = 1.0 + tanh
    act = half * twice_sig
    slope_ref[...] = 0.5 * (twice_sig + act * (1.0 - tanh))
    gate = act[:, :width]
    gate_ref[...] = gate
    dz = mgrad * gate
    for h in range(HEADS):
        lo = h * head
        send_ref[h] = jnp.concatenate(
            [
                act[:, 2 * width + lo : 2 * width + lo + head],
                act[:, 3 * width + lo : 3 * width + lo + head],
                act[:, width + lo : width + lo + head],
                dz[:, lo : lo + head],
            ],
            axis=1,
        ).astype(bf16)


def weight_tile(keys, half_queries_t):
    half = dot(keys, half_queries_t)
    tanh = jnp.tanh(half)
    twice_sig = 1.0 + tanh
    wgt = half * twice_sig
    return wgt, twice_sig + wgt * (1.0 - tanh)


def causal_mask(rows):
    return iota((rows, rows), 0) <= iota((rows, rows), 1)


def forward_kernel(ready, x_ref, att_ref, dz_ref, share_ref, *refs):
    if ready:
        wgt_ref, slope_ref = refs[:2]
    vt_scr, stat_ref = refs[-2:]
    blocks, rows, cols = x_ref.shape
    head = cols // 4
    scale = head ** (-0.5)
    causal = causal_mask(rows)
    place = 0
    for b in range(blocks):
        queries_t = (x_ref[b, :, 0:head].astype(f32) * (0.5 * scale)).T.astype(bf16)
        vt_scr[b] = x_ref[b, :, 2 * head : 3 * head].astype(f32).T.astype(bf16)
        att = jnp.zeros((head, rows), f32)
        for c in range(b + 1):
            wgt, slope = weight_tile(x_ref[c, :, head : 2 * head], queries_t)
            if b == c:
                wgt = jnp.where(causal, wgt, 0.0)
                slope = jnp.where(causal, slope, 0.0)
            wgt = wgt.astype(bf16)
            att = att + dot(vt_scr[c], wgt)
            if ready:
                wgt_ref[place] = wgt
                slope_ref[place] = slope
            place += 1
        dz = x_ref[b, :, 3 * head :].astype(f32).T
        att_ref[b] = att
        dz_ref[b] = dz
        mean = jnp.sum(att, axis=0, keepdims=True) * (1.0 / head)
        cent = att - mean
        stat_ref[0, b : b + 1, :] = mean
        stat_ref[1, b : b + 1, :] = jnp.sum(cent * cent, axis=0, keepdims=True)
        stat_ref[2, b : b + 1, :] = jnp.sum(dz, axis=0, keepdims=True)
        stat_ref[3, b : b + 1, :] = jnp.sum(cent * dz, axis=0, keepdims=True)
    mean = stat_ref[0]
    high = mean.astype(bf16)
    low = (mean - high.astype(f32)).astype(bf16)
    others = [stat_ref[n].astype(bf16) for n in range(1, 4)]
    for g in range(blocks):
        for n, stat in enumerate([high, low] + others):
            share_ref[g, n] = stat


def backward_kernel(copies, ready, *refs):
    if ready:
        x_ref, wgt_ref, slope_ref, att_ref, dz_ref, stats_ref, out_ref = refs[:7]
        dq_scr, da_scr, dat_scr, q_scr = refs[7:]
    else:
        x_ref, att_ref, dz_ref, stats_ref, out_ref = refs[:5]
        dq_scr, da_scr, dat_scr, q_scr, qt_scr = refs[5:]
    blocks, rows, cols = x_ref.shape
    head = cols // 4
    scale = head ** (-0.5)
    width = head * HEADS
    heads = range(0, HEADS * copies, copies)

    def stat_of(h, n):
        return stats_ref[h, n].astype(f32)

    means = {h: stat_of(h, 0) + stat_of(h, 1) for h in heads}
    mean = sum(means.values()) * (1.0 / HEADS)
    square = 0.0
    dz_sum = 0.0
    dz_att = 0.0
    for h in heads:
        off = means[h] - mean
        square = square + (stat_of(h, 2) + head * (off * off))
        dz_sum = dz_sum + stat_of(h, 3)
        dz_att = dz_att + (stat_of(h, 4) + stat_of(h, 3) * off)
    inv = 1.0 / jnp.sqrt(square * (1.0 / width) + eps_norm)
    mean_dz = dz_sum * (1.0 / width)
    mean_prod = dz_att * inv * (1.0 / width)
    for b in range(blocks):
        att_n = (att_ref[b] - mean[b : b + 1]) * inv[b : b + 1]
        da_t = (dz_ref[b] - mean_dz[b : b + 1] - att_n * mean_prod[b : b + 1]) * inv[b : b + 1]
        out_ref[b, :, 3 * head :] = att_n.T.astype(bf16)
        dat_scr[b] = (0.5 * da_t).astype(bf16)
        da_scr[b] = da_t.T.astype(bf16)
        q = x_ref[b, :, 0:head].astype(f32) * scale
        q_scr[b] = q.astype(bf16)
        if not ready:
            qt_scr[b] = (0.5 * q).T.astype(bf16)
    causal = causal_mask(rows)
    for c in range(blocks):
        keys = x_ref[c, :, head : 2 * head]
        keys_t = keys.astype(f32).T.astype(bf16)
        values = x_ref[c, :, 2 * head : 3 * head]
        dk = jnp.zeros((rows, head), f32)
        dv = jnp.zeros((rows, head), f32)
        for b in range(c, blocks):
            if ready:
                place = b * (b + 1) // 2 + c
                wgt = wgt_ref[place]
                slope = slope_ref[place]
            else:
                wgt, slope = weight_tile(keys, qt_scr[b])
                if b == c:
                    wgt = jnp.where(causal, wgt, 0.0)
                    slope = jnp.where(causal, slope, 0.0)
                wgt = wgt.astype(bf16)
            sgrad = (dot(values, dat_scr[b]) * slope).astype(bf16)
            dv = dv + dot(wgt, da_scr[b])
            dk = dk + dot(sgrad, q_scr[b])
            part = dot(keys_t, sgrad)
            if c == 0:
                dq_scr[b] = part
            else:
                dq_scr[b] = dq_scr[b] + part
        out_ref[c, :, head : 2 * head] = dk.astype(bf16)
        out_ref[c, :, 2 * head : 3 * head] = dv.astype(bf16)
        out_ref[c, :, 0:head] = (dq_scr[c] * scale).T.astype(bf16)


def head_columns(grad_ref, copies, part, head):
    return jnp.concatenate(
        [
            grad_ref[h * copies, :, part * head : (part + 1) * head].astype(f32)
            for h in range(HEADS)
        ],
        axis=1,
    )


def finish_kernel(
    copies,
    mail_ref,
    grad_ref,
    slope_ref,
    gate_ref,
    mgrad_ref,
    emb_ref,
    cot_ref,
    w_ref,
    wo_ref,
    out_ref,
    layer_ref,
):
    slot_row, live_row = read_note(mail_ref)
    count, width = emb_ref.shape
    slots = out_ref.shape[0]
    head = width // HEADS
    live_col = to_col(live_row)
    columns = functools.partial(head_columns, grad_ref, copies, head=head)
    att_n = columns(3)
    mixed = (att_n * gate_ref[...]).astype(bf16)
    branch = dot(mixed, wo_ref[...])
    embedded = emb_ref[...].astype(f32)
    layer_ref[...] = (live_col * (embedded + branch)).astype(bf16)
    act_grad = jnp.concatenate(
        [mgrad_ref[...] * att_n, columns(2), columns(0), columns(1)], axis=1
    )
    pre_grad = (act_grad * slope_ref[...]).astype(bf16)
    norm_grad = dot(pre_grad, w_ref[...], ((1,), (1,)))
    normed, spread = normalize(embedded)
    mean_grad = jnp.mean(norm_grad, axis=-1, keepdims=True)
    mean_prod = jnp.mean(norm_grad * normed, axis=-1, keepdims=True)
    cot = jnp.where(live_col > 0.0, cot_ref[...].astype(f32), 0.0)
    emb_grad = cot + (norm_grad - mean_grad - normed * mean_prod) / spread
    places = jnp.where(iota((slots, count), 0) == slot_row, 1.0, 0.0).astype(bf16)
    out_ref[...] = dot(places, emb_grad.astype(bf16)).astype(bf16)


def pick_kernel(
    cap, part, askers, mail_ref, table_hbm, out_ref, table_ref, lane_scr, block_scr, sems
):
    chunks, chunk, width = table_ref.shape
    slots = out_ref.shape[0]

    def fetch(n):
        return pltpu.make_async_copy(
            table_hbm.at[pl.ds(n * chunk, chunk), :], table_ref.at[n], sems.at[n]
        )

    for n in range(chunks):
        fetch(n).start()
    wish = mail_ref[:, :LANES].astype(f32).T
    for taker, asker in enumerate(askers):
        column = jnp.maximum(wish[:cap, asker : asker + 1], 0.0)
        block = jnp.floor(column * (1.0 / part))
        place = slice(taker * cap, (taker + 1) * cap)
        block_scr[place, :] = jnp.broadcast_to(block, (cap, part))
        lane_scr[place, :] = jnp.broadcast_to(column - block * part, (cap, part))
    block = block_scr[...].astype(bf16)
    ramp = iota((slots, part), 1).astype(f32).astype(bf16)
    one = jnp.ones((), bf16)
    zero = jnp.zeros((), bf16)
    lanes = jnp.where(lane_scr[...].astype(bf16) == ramp, one, zero)
    total = jnp.zeros((slots, width), f32)
    for n in range(chunks):
        fetch(n).wait()
        for m in range(chunk // part):
            picks = jnp.where(block == n * (chunk // part) + m, lanes, zero)
            total = total + dot(picks, table_ref[n, m * part : (m + 1) * part, :])
    out_ref[...] = total.astype(bf16)


def table_kernel(part, asked_ref, arrived_ref, layer_ref, out_ref, copy_ref, picks_scr):
    rows = out_ref.shape[0]
    slots = arrived_ref.shape[0]

    @pl.when(pl.program_id(0) == 0)
    def unused():
        copy_ref[...] = layer_ref[...]

    local_row = asked_ref[...] - pl.program_id(0) * rows
    ramp = iota((part, slots), 0).astype(f32).astype(bf16)
    for start in range(0, rows, part):
        near_row = local_row - start
        inside = (near_row >= 0) & (near_row < part)
        near_row = jnp.where(inside, near_row, -1).astype(f32)
        near_row = jnp.broadcast_to(near_row, (16, slots)).astype(bf16)[0:1]
        picks = jnp.where(ramp == near_row, jnp.ones((), bf16), jnp.zeros((), bf16))
        picks_scr[start : start + part, :] = picks
    out_ref[...] = dot(picks_scr[...], arrived_ref[...]).astype(bf16)


def all_to_all(pieces, axes):
    return lax.all_to_all(pieces, axes, split_axis=0, concat_axis=0, tiled=True)


def local(item_ids, history_len, row_place, item_table, input_proj, output_proj, out_cotangent):
    count = item_ids.shape[1]
    rows_dev, width = item_table.shape
    outer = lax.axis_size("a")
    inner = lax.axis_size("d")
    owners = 4 * outer * inner
    group = 2 * inner
    copies = group // HEADS
    cap = 3 * count // owners
    slots = owners * cap
    head = width // HEADS
    part = math.gcd(rows_dev, 256)
    moved = functools.partial(
        lax.ppermute, axis_name=SWAPPED, perm=[(0, 0), (1, 2), (2, 1), (3, 3)]
    )
    askers = tuple(
        ((a * 2 + c) * 2 + b) * inner + d
        for a in range(outer)
        for b in range(2)
        for c in range(2)
        for d in range(inner)
    )
    at_a, at_b, at_c, at_d = (lax.axis_index(name) for name in ALL)

    def number(value):
        return value.reshape(1).astype(i32)

    def swapped(pieces):
        shape = pieces.shape
        parts = pieces.reshape((outer, 2, 2, inner) + shape[1:])
        return jnp.swapaxes(parts, 1, 2).reshape(shape)

    cot = moved(out_cotangent[0])
    mail = pl.pallas_call(
        functools.partial(request_kernel, rows_dev, cap),
        out_shape=pltpu.VMEM((owners, LANES + count), i32),
        in_specs=[smem()] * 3 + [hbm()] * 2,
        out_specs=vmem(),
        scratch_shapes=[
            pltpu.SMEM((1, count), i32),
            pltpu.VMEM((1, count), i32),
            pltpu.VMEM((row_place.shape[0] // LANES, LANES), i32),
            pltpu.VMEM((count, LANES), i32),
            pltpu.SemaphoreType.DMA((3,)),
        ],
        compiler_params=params(),
        name="requests",
    )(
        number((at_c * inner + at_d) * count),
        number(((at_a * 2 + at_c) * 2 + at_b) * inner + at_d),
        history_len,
        far(item_ids),
        far(row_place.reshape(-1, LANES)),
    )
    mail = all_to_all(mail, ALL)
    wanted = swapped(mail[:, :cap]).reshape(1, slots)
    chunks = min(4, rows_dev // part)
    rows = pl.pallas_call(
        functools.partial(pick_kernel, cap, part, askers),
        out_shape=pltpu.VMEM((slots, width), bf16),
        in_specs=[vmem(), hbm()],
        out_specs=vmem(),
        scratch_shapes=[
            pltpu.VMEM((chunks, rows_dev // chunks, width), bf16),
            pltpu.VMEM((slots, part), f32),
            pltpu.VMEM((slots, part), f32),
            pltpu.SemaphoreType.DMA((chunks,)),
        ],
        compiler_params=params(),
        name="pick",
    )(near(mail), far(item_table))
    rows = all_to_all(rows.reshape(owners, cap, width), ALL).reshape(slots, width)

    send, emb, slope, gate, mgrad = kernel_call(
        project_kernel,
        (
            ((HEADS, count, 4 * head), bf16),
            ((count, width), bf16),
            ((count, 4 * width), f32),
            ((count, width), f32),
            ((count, width), f32),
        ),
        (mail, rows, cot, input_proj, output_proj),
    )
    if copies > 1:
        send = jnp.repeat(send, copies, axis=0)
    mine = all_to_all(send, GROUP)
    tiles = group * (group + 1) // 2
    ready = tiles * count * count * 6 <= 16 * 1024 * 1024
    att, dz, share, *weights = kernel_call(
        functools.partial(forward_kernel, ready),
        (
            ((group, head, count), f32),
            ((group, head, count), f32),
            ((group, 5, group, count), bf16),
        )
        + (((tiles, count, count), bf16), ((tiles, count, count), f32)) * ready,
        (mine,),
        scratch=[
            pltpu.VMEM((group, head, count), bf16),
            pltpu.VMEM((4, group, count), f32),
        ],
    )
    stats = all_to_all(share, GROUP)
    scratch = [
        pltpu.VMEM((group, head, count), f32),
        pltpu.VMEM((group, count, head), bf16),
        pltpu.VMEM((group, head, count), bf16),
        pltpu.VMEM((group, count, head), bf16),
    ]
    if not ready:
        scratch.append(pltpu.VMEM((group, head, count), bf16))
    (grads,) = kernel_call(
        functools.partial(backward_kernel, copies, ready),
        (((group, count, 4 * head), bf16),),
        (mine, *weights, att, dz, stats),
        scratch=scratch,
    )
    back = all_to_all(grads, GROUP)
    outgoing, layer_out = kernel_call(
        functools.partial(finish_kernel, copies),
        (((slots, width), bf16), ((count, width), bf16)),
        (mail, back, slope, gate, mgrad, emb, cot, input_proj, output_proj),
    )
    arrived = all_to_all(outgoing.reshape(owners, cap, width), ALL).reshape(slots, width)
    layer_out = moved(layer_out)
    tile = math.gcd(rows_dev, 1024)
    table_grad, layer_out = pl.pallas_call(
        functools.partial(table_kernel, part),
        out_shape=(
            jax.ShapeDtypeStruct((rows_dev, width), bf16),
            jax.ShapeDtypeStruct((count, width), bf16),
        ),
        grid=(rows_dev // tile,),
        in_specs=[vmem(), vmem(), vmem()],
        out_specs=(
            pl.BlockSpec((tile, width), lambda r: (r, 0)),
            pl.BlockSpec((count, width), lambda r: (0, 0)),
        ),
        scratch_shapes=[pltpu.VMEM((tile, slots), bf16)],
        compiler_params=params(),
        name="table_grad",
    )(near(wanted), near(arrived), near(layer_out))
    return (layer_out[None], table_grad)


def solution(mesh):
    table, seq = mesh.shape["table"], mesh.shape["seq"]
    if table % 2 or seq % 2 or seq % HEADS:
        raise ValueError("unsupported mesh")
    finer = Mesh(mesh.devices.reshape(table // 2, 2, 2, seq // 2), ALL)
    placed = (
        P(("a", "b"), ("c", "d")),
        P(("a", "b")),
        P(),
        P(ALL, None),
        P(),
        P(),
        P(("a", "b"), ("c", "d"), None),
    )

    return jax.shard_map(
        local,
        mesh=finer,
        in_specs=placed,
        out_specs=(P(("a", "b"), ("c", "d"), None), P(ALL, None)),
        check_vma=False,
    )
```

```python
import functools
import math

import jax
import jax.numpy as jnp
from jax import lax
from jax.experimental import pallas as pl
from jax.experimental.pallas import tpu as pltpu
from jax.sharding import Mesh, PartitionSpec as P

HEADS = 8
eps_norm = 1e-05
LANES = 128
TILE = 1024
ALL = ("a", "b", "c", "d")
GROUP = ("b", "d")
SWAPPED = ("b", "c")
f32 = jnp.float32
bf16 = jnp.bfloat16
i32 = jnp.int32


def vmem():
    return pl.BlockSpec(memory_space=pltpu.VMEM)


def smem():
    return pl.BlockSpec(memory_space=pltpu.SMEM)


def params():
    return pltpu.CompilerParams(vmem_limit_bytes=24 * 1024 * 1024)


def near(array):
    return pltpu.with_memory_space_constraint(array, pltpu.VMEM)


def far(array):
    return pltpu.with_memory_space_constraint(array, pltpu.HBM)


def hbm():
    return pl.BlockSpec(memory_space=pltpu.HBM)


def kernel_call(kernel, outs, args, scratch=(), numbers=()):
    return pl.pallas_call(
        kernel,
        out_shape=tuple(pltpu.VMEM(shape, dtype) for shape, dtype in outs),
        in_specs=[smem()] * len(numbers) + [vmem()] * len(args),
        out_specs=tuple(vmem() for unused in outs),
        scratch_shapes=list(scratch),
        compiler_params=params(),
    )(*numbers, *map(near, args))


def dot(lhs, rhs, dims=((1,), (0,))):
    return lax.dot_general(lhs, rhs, (dims, ((), ())), preferred_element_type=f32)


def iota(shape, axis):
    return lax.broadcasted_iota(i32, shape, axis)


def to_col(row):
    size = row.shape[1]
    same = iota((size, size), 0) == iota((size, size), 1)
    return jnp.sum(jnp.where(same, row, 0.0), axis=1, keepdims=True)


def to_row(col):
    size = col.shape[0]
    same = iota((size, size), 0) == iota((size, size), 1)
    return jnp.sum(jnp.where(same, col, 0.0), axis=0, keepdims=True)


def request_kernel(
    rows_dev,
    cap,
    unused_s,
    block_s,
    twin_s,
    length_s,
    ids_hbm,
    place_hbm,
    table_hbm,
    mail_ref,
    table_ref,
    ids_s,
    ids_ref,
    place_ref,
    rows_scr,
    sems,
):
    count = ids_ref.shape[1]
    copies = [
        pltpu.make_async_copy(source, target, sems.at[n])
        for n, (source, target) in enumerate(
            [
                (ids_hbm, ids_s),
                (ids_hbm, ids_ref),
                (place_hbm, place_ref),
                (table_hbm, table_ref),
            ]
        )
    ]
    for copy in copies:
        copy.start()
    for copy in copies[:3]:
        copy.wait()

    def fetch(step, unused):
        rows_scr[pl.ds(step, 1), :] = place_ref[pl.ds(ids_s[0, step] >> 7, 1), :]
        return unused

    lax.fori_loop(0, count, fetch, 0, unroll=8)
    lane_col = to_col((ids_ref[...] & (LANES - 1)).astype(f32)).astype(i32)
    lanes = iota((count, LANES), 1)
    stored = jnp.sum(
        jnp.where(lanes == lane_col, rows_scr[...].astype(f32), 0.0), axis=1, keepdims=True
    ).astype(i32)
    shift = rows_dev.bit_length() - 1
    owner = stored >> shift
    local_row = stored & (rows_dev - 1)
    hits = lanes == owner
    hits_f = jnp.where(hits, 1.0, 0.0)
    before = jnp.where(iota((count, count), 1) < iota((count, count), 0), 1.0, 0.0)
    earlier = dot(before.astype(bf16), hits_f.astype(bf16))
    rank = jnp.sum(jnp.where(hits, earlier, 0.0), axis=1, keepdims=True)
    in_rank = lanes == rank.astype(i32)
    asked = local_row + 1
    high = jnp.where(in_rank, (asked >> 7).astype(f32), 0.0).astype(bf16)
    low = jnp.where(in_rank, (asked & 127).astype(f32), 0.0).astype(bf16)
    hits_t = hits_f.T.astype(bf16)
    owners = mail_ref.shape[0]
    wish = dot(hits_t, high) * 128.0 + dot(hits_t, low)
    mail_ref[:, :LANES] = wish[:owners].astype(i32) - 1
    slot = owner.astype(f32) * cap + rank
    live = (block_s[0] * count + iota((1, count), 1)) < length_s[0]
    note = to_row(slot).astype(i32) * 2 + jnp.where(live, 1, 0)
    mail_ref[:, LANES:] = jnp.where(iota((owners, count), 0) == twin_s[0], note, 0)
    copies[3].wait()


def read_note(mail_ref):
    note = jnp.sum(mail_ref[:, LANES:].astype(f32), axis=0, keepdims=True).astype(i32)
    return note >> 1, (note & 1).astype(f32)


def normalize(inputs):
    centred = inputs - jnp.mean(inputs, axis=-1, keepdims=True)
    spread = jnp.sqrt(jnp.mean(centred * centred, axis=-1, keepdims=True) + eps_norm)
    return (centred / spread, spread)


def hand_out(me_s, pieces, source_ref, copies=1):
    for k, piece in enumerate(pieces):
        piece[...] = source_ref[jnp.bitwise_xor(me_s[0], k) // copies]


def take_in(me_s, pieces, target_ref):
    for k, piece in enumerate(pieces):
        target_ref[jnp.bitwise_xor(me_s[0], k)] = piece[...]


def project_kernel(
    copies, me_s, mail_ref, rows_ref, cot_ref, w_ref, wo_ref, emb_ref, slope_ref, gate_ref, mgrad_ref, *refs
):
    pieces, send_ref = refs[:-1], refs[-1]
    slot_row, live_row = read_note(mail_ref)
    count = slot_row.shape[1]
    slots, width = rows_ref.shape
    head = width // HEADS
    slot_col = to_col(slot_row.astype(f32)).astype(i32)
    live_col = to_col(live_row)
    picks = jnp.where(iota((count, slots), 1) == slot_col, 1.0, 0.0).astype(bf16)
    embedded = dot(picks, rows_ref[...])
    emb_ref[...] = embedded.astype(bf16)
    normed, _ = normalize(embedded)
    pre = dot(normed.astype(bf16), w_ref[...])
    cot = jnp.where(live_col > 0.0, cot_ref[...].astype(f32), 0.0).astype(bf16)
    mgrad = dot(cot, wo_ref[...], ((1,), (1,)))
    mgrad_ref[...] = mgrad
    half = 0.5 * pre
    tanh = jnp.tanh(half)
    twice_sig = 1.0 + tanh
    act = half * twice_sig
    slope_ref[...] = 0.5 * (twice_sig + act * (1.0 - tanh))
    gate = act[:, :width]
    gate_ref[...] = gate
    dz = mgrad * gate
    for h in range(HEADS):
        lo = h * head
        send_ref[h] = jnp.concatenate(
            [
                act[:, 2 * width + lo : 2 * width + lo + head],
                act[:, 3 * width + lo : 3 * width + lo + head],
                act[:, width + lo : width + lo + head],
                dz[:, lo : lo + head],
            ],
            axis=1,
        ).astype(bf16)
    hand_out(me_s, pieces, send_ref, copies)


def weight_tile(keys, half_queries_t):
    half = dot(keys, half_queries_t)
    tanh = jnp.tanh(half)
    twice_sig = 1.0 + tanh
    wgt = half * twice_sig
    return wgt, twice_sig + wgt * (1.0 - tanh)


def causal_mask(rows):
    return iota((rows, rows), 0) <= iota((rows, rows), 1)


def forward_kernel(ready, group, me_s, *refs):
    pieces, refs = refs[:group], refs[group:]
    x_ref, att_ref, dz_ref, share_ref, wgt_ref = refs[:5]
    slope_ref = refs[5] if ready else None
    vt_scr, keys_scr, stat_ref = refs[-3:]
    take_in(me_s, pieces, x_ref)
    blocks, rows, cols = x_ref.shape
    head = cols // 4
    scale = head ** (-0.5)
    causal = causal_mask(rows)
    for b in range(blocks):
        span = slice(b * rows, (b + 1) * rows)
        keys_scr[span, :] = x_ref[b, :, head : 2 * head]
        vt_scr[:, span] = x_ref[b, :, 2 * head : 3 * head].astype(f32).T.astype(bf16)
    for b in range(blocks):
        queries_t = (x_ref[b, :, 0:head].astype(f32) * (0.5 * scale)).T.astype(bf16)
        above = b * rows
        upto = above + rows
        wgt, slope = weight_tile(keys_scr[:upto, :], queries_t)
        place = b * (b + 1) // 2 * rows
        if above:
            wgt_ref[place : place + above, :] = wgt[:above].astype(bf16)
        wgt_ref[place + above : place + upto, :] = jnp.where(causal, wgt[above:], 0.0).astype(bf16)
        if ready:
            if above:
                slope_ref[place : place + above, :] = slope[:above]
            slope_ref[place + above : place + upto, :] = jnp.where(causal, slope[above:], 0.0)
        att = dot(vt_scr[:, :upto], wgt_ref[place : place + upto, :])
        dz = x_ref[b, :, 3 * head :].astype(f32).T
        att_ref[b] = att
        dz_ref[b] = dz
        mean = jnp.sum(att, axis=0, keepdims=True) * (1.0 / head)
        cent = att - mean
        stat_ref[0, b : b + 1, :] = mean
        stat_ref[1, b : b + 1, :] = jnp.sum(cent * cent, axis=0, keepdims=True)
        stat_ref[2, b : b + 1, :] = jnp.sum(dz, axis=0, keepdims=True)
        stat_ref[3, b : b + 1, :] = jnp.sum(cent * dz, axis=0, keepdims=True)
    mean = stat_ref[0]
    high = mean.astype(bf16)
    low = (mean - high.astype(f32)).astype(bf16)
    others = [stat_ref[n].astype(bf16) for n in range(1, 4)]
    for g in range(blocks):
        for n, stat in enumerate([high, low] + others):
            share_ref[g, n] = stat


def backward_kernel(copies, ready, group, me_s, *refs):
    if ready:
        x_ref, wgt_ref, slope_ref, att_ref, dz_ref, stats_ref = refs[:6]
    else:
        x_ref, wgt_ref, att_ref, dz_ref, stats_ref = refs[:5]
        qt_scr = refs[-1]
    refs = refs[5 + ready :]
    pieces = refs[:group]
    out_ref, da_scr, dat_scr, q_scr, keys_scr, keyst_scr, values_scr, dk_scr, dv_scr = refs[
        group : group + 9
    ]
    blocks, rows, cols = x_ref.shape
    head = cols // 4
    scale = head ** (-0.5)
    width = head * HEADS
    heads = range(0, HEADS * copies, copies)

    def stat_of(h, n):
        return stats_ref[h, n].astype(f32)

    means = {h: stat_of(h, 0) + stat_of(h, 1) for h in heads}
    mean = sum(means.values()) * (1.0 / HEADS)
    square = 0.0
    dz_sum = 0.0
    dz_att = 0.0
    for h in heads:
        off = means[h] - mean
        square = square + (stat_of(h, 2) + head * (off * off))
        dz_sum = dz_sum + stat_of(h, 3)
        dz_att = dz_att + (stat_of(h, 4) + stat_of(h, 3) * off)
    inv = 1.0 / jnp.sqrt(square * (1.0 / width) + eps_norm)
    mean_dz = dz_sum * (1.0 / width)
    mean_prod = dz_att * inv * (1.0 / width)
    for b in range(blocks):
        att_n = (att_ref[b] - mean[b : b + 1]) * inv[b : b + 1]
        da_t = (dz_ref[b] - mean_dz[b : b + 1] - att_n * mean_prod[b : b + 1]) * inv[b : b + 1]
        out_ref[b, :, 3 * head :] = att_n.T.astype(bf16)
        dat_scr[b] = (0.5 * da_t).astype(bf16)
        da_scr[b] = da_t.T.astype(bf16)
        q = x_ref[b, :, 0:head].astype(f32) * scale
        q_scr[b] = q.astype(bf16)
        if not ready:
            qt_scr[b] = (0.5 * q).T.astype(bf16)
    causal = causal_mask(rows)
    for b in range(blocks):
        span = slice(b * rows, (b + 1) * rows)
        keys = x_ref[b, :, head : 2 * head]
        keys_scr[span, :] = keys
        keyst_scr[:, span] = keys.astype(f32).T.astype(bf16)
        values_scr[span, :] = x_ref[b, :, 2 * head : 3 * head]
    for b in range(blocks):
        above = b * rows
        upto = above + rows
        place = b * (b + 1) // 2 * rows
        wgt = wgt_ref[place : place + upto, :]
        if ready:
            slope = slope_ref[place : place + upto, :]
        else:
            _, slope = weight_tile(keys_scr[:upto, :], qt_scr[b])
        sgrad = dot(values_scr[:upto, :], dat_scr[b]) * slope
        if not ready:
            mask = iota((upto, rows), 0) <= iota((upto, rows), 1) + above
            sgrad = jnp.where(mask, sgrad, 0.0)
        sgrad = sgrad.astype(bf16)
        dv = dot(wgt, da_scr[b])
        dk = dot(sgrad, q_scr[b])
        if above:
            dv_scr[:above, :] = dv_scr[:above, :] + dv[:above]
            dk_scr[:above, :] = dk_scr[:above, :] + dk[:above]
        dv_scr[above:upto, :] = dv[above:]
        dk_scr[above:upto, :] = dk[above:]
        dq = dot(keyst_scr[:, :upto], sgrad)
        out_ref[b, :, 0:head] = (dq * scale).T.astype(bf16)
    for b in range(blocks):
        span = slice(b * rows, (b + 1) * rows)
        out_ref[b, :, head : 2 * head] = dk_scr[span, :].astype(bf16)
        out_ref[b, :, 2 * head : 3 * head] = dv_scr[span, :].astype(bf16)
    hand_out(me_s, pieces, out_ref)


def head_columns(grad_ref, copies, part, head):
    return jnp.concatenate(
        [
            grad_ref[h * copies, :, part * head : (part + 1) * head].astype(f32)
            for h in range(HEADS)
        ],
        axis=1,
    )


def finish_kernel(copies, group, me_s, *refs):
    pieces, refs = refs[:group], refs[group:]
    mail_ref, slope_ref, gate_ref, mgrad_ref, emb_ref, cot_ref, w_ref, wo_ref = refs[:8]
    out_ref, layer_ref, grad_ref = refs[8:]
    take_in(me_s, pieces, grad_ref)
    slot_row, live_row = read_note(mail_ref)
    count, width = emb_ref.shape
    slots = out_ref.shape[0]
    head = width // HEADS
    live_col = to_col(live_row)
    columns = functools.partial(head_columns, grad_ref, copies, head=head)
    att_n = columns(3)
    mixed = (att_n * gate_ref[...]).astype(bf16)
    branch = dot(mixed, wo_ref[...])
    embedded = emb_ref[...].astype(f32)
    layer_ref[...] = (live_col * (embedded + branch)).astype(bf16)
    act_grad = jnp.concatenate(
        [mgrad_ref[...] * att_n, columns(2), columns(0), columns(1)], axis=1
    )
    pre_grad = (act_grad * slope_ref[...]).astype(bf16)
    norm_grad = dot(pre_grad, w_ref[...], ((1,), (1,)))
    normed, spread = normalize(embedded)
    mean_grad = jnp.mean(norm_grad, axis=-1, keepdims=True)
    mean_prod = jnp.mean(norm_grad * normed, axis=-1, keepdims=True)
    cot = jnp.where(live_col > 0.0, cot_ref[...].astype(f32), 0.0)
    emb_grad = cot + (norm_grad - mean_grad - normed * mean_prod) / spread
    places = jnp.where(iota((slots, count), 0) == slot_row, 1.0, 0.0).astype(bf16)
    out_ref[...] = dot(places, emb_grad.astype(bf16)).astype(bf16)


def pick_kernel(cap, part, askers, mail_ref, table_ref, out_ref, lane_scr, block_scr):
    rows, width = table_ref.shape
    slots = out_ref.shape[0]
    wish = mail_ref[:, :LANES].astype(f32).T
    for taker, asker in enumerate(askers):
        column = jnp.maximum(wish[:cap, asker : asker + 1], 0.0)
        block = jnp.floor(column * (1.0 / part))
        place = slice(taker * cap, (taker + 1) * cap)
        block_scr[place, :] = jnp.broadcast_to(block, (cap, part))
        lane_scr[place, :] = jnp.broadcast_to(column - block * part, (cap, part))
    block = block_scr[...].astype(bf16)
    ramp = iota((slots, part), 1).astype(f32).astype(bf16)
    one = jnp.ones((), bf16)
    zero = jnp.zeros((), bf16)
    lanes = jnp.where(lane_scr[...].astype(bf16) == ramp, one, zero)
    total = jnp.zeros((slots, width), f32)
    for n in range(rows // part):
        picks = jnp.where(block == n, lanes, zero)
        total = total + dot(picks, table_ref[n * part : (n + 1) * part, :])
    out_ref[...] = total.astype(bf16)


def table_kernel(part, asked_ref, arrived_ref, layer_ref, out_hbm, copy_hbm, out_scr, picks_scr, sems):
    chunks, chunk, _ = out_scr.shape
    slots = arrived_ref.shape[0]
    finished = pltpu.make_async_copy(layer_ref, copy_hbm, sems.at[chunks])
    finished.start()
    ramp = iota((part, slots), 0).astype(f32).astype(bf16)
    copies = []
    for n in range(chunks):
        for start in range(0, chunk, part):
            near_row = asked_ref[...] - (n * chunk + start)
            inside = (near_row >= 0) & (near_row < part)
            near_row = jnp.where(inside, near_row, -1).astype(f32)
            near_row = jnp.broadcast_to(near_row, (16, slots)).astype(bf16)[0:1]
            picks = jnp.where(ramp == near_row, jnp.ones((), bf16), jnp.zeros((), bf16))
            picks_scr[n % 2, start : start + part, :] = picks
        out_scr[n] = dot(picks_scr[n % 2], arrived_ref[...]).astype(bf16)
        copy = pltpu.make_async_copy(
            out_scr.at[n], out_hbm.at[pl.ds(n * chunk, chunk), :], sems.at[n]
        )
        copy.start()
        copies.append(copy)
    for copy in copies:
        copy.wait()
    finished.wait()


def all_to_all(pieces, axes):
    return lax.all_to_all(pieces, axes, split_axis=0, concat_axis=0, tiled=True)


def local(item_ids, history_len, row_place, item_table, input_proj, output_proj, out_cotangent):
    count = item_ids.shape[1]
    rows_dev, width = item_table.shape
    outer = lax.axis_size("a")
    inner = lax.axis_size("d")
    owners = 4 * outer * inner
    group = 2 * inner
    copies = group // HEADS
    cap = 3 * count // owners
    slots = owners * cap
    head = width // HEADS
    part = math.gcd(rows_dev, 256)
    moved = functools.partial(
        lax.ppermute, axis_name=SWAPPED, perm=[(0, 0), (1, 2), (2, 1), (3, 3)]
    )
    askers = tuple(
        ((a * 2 + c) * 2 + b) * inner + d
        for a in range(outer)
        for b in range(2)
        for c in range(2)
        for d in range(inner)
    )
    at_a, at_b, at_c, at_d = (lax.axis_index(name) for name in ALL)

    def number(value):
        return value.reshape(1).astype(i32)

    me = number(at_b * inner + at_d)

    def swapped(pieces):
        shape = pieces.shape
        parts = pieces.reshape((outer, 2, 2, inner) + shape[1:])
        return jnp.swapaxes(parts, 1, 2).reshape(shape)

    cot = moved(out_cotangent[0])
    mail, table = pl.pallas_call(
        functools.partial(request_kernel, rows_dev, cap),
        out_shape=(
            pltpu.VMEM((owners, LANES + count), i32),
            pltpu.VMEM(item_table.shape, bf16),
        ),
        in_specs=[smem()] * 4 + [hbm()] * 3,
        out_specs=(vmem(), vmem()),
        scratch_shapes=[
            pltpu.SMEM((1, count), i32),
            pltpu.VMEM((1, count), i32),
            pltpu.VMEM((row_place.shape[0] // LANES, LANES), i32),
            pltpu.VMEM((count, LANES), i32),
            pltpu.SemaphoreType.DMA((4,)),
        ],
        compiler_params=params(),
        name="requests",
    )(
        me,
        number(at_c * inner + at_d),
        number(((at_a * 2 + at_c) * 2 + at_b) * inner + at_d),
        history_len,
        far(item_ids),
        far(row_place.reshape(-1, LANES)),
        far(item_table),
    )
    mail = all_to_all(mail, ALL)
    wanted = swapped(mail[:, :cap]).reshape(1, slots)
    (rows,) = kernel_call(
        functools.partial(pick_kernel, cap, part, askers),
        (((slots, width), bf16),),
        (mail, table),
        scratch=[pltpu.VMEM((slots, part), f32), pltpu.VMEM((slots, part), f32)],
    )
    rows = all_to_all(rows.reshape(owners, cap, width), ALL).reshape(slots, width)

    piece = ((count, 4 * head), bf16)
    whole = pltpu.VMEM((group, count, 4 * head), bf16)

    def exchange(pieces):
        return [pieces[0]] + [
            lax.ppermute(pieces[k], GROUP, [(g, g ^ k) for g in range(group)])
            for k in range(1, group)
        ]

    emb, slope, gate, mgrad, *sent = kernel_call(
        functools.partial(project_kernel, copies),
        (
            ((count, width), bf16),
            ((count, 4 * width), f32),
            ((count, width), f32),
            ((count, width), f32),
        )
        + (piece,) * group,
        (mail, rows, cot, input_proj, output_proj),
        scratch=[pltpu.VMEM((HEADS, count, 4 * head), bf16)],
        numbers=(me,),
    )
    mine = exchange(sent)
    length = group * count
    tiles = group * (group + 1) // 2 * count
    ready = tiles * count * 6 <= 16 * 1024 * 1024
    x, att, dz, share, *weights = kernel_call(
        functools.partial(forward_kernel, ready, group),
        (
            ((group, count, 4 * head), bf16),
            ((group, head, count), f32),
            ((group, head, count), f32),
            ((group, 5, group, count), bf16),
        )
        + (((tiles, count), bf16),)
        + (((tiles, count), f32),) * ready,
        mine,
        scratch=[
            pltpu.VMEM((head, length), bf16),
            pltpu.VMEM((length, head), bf16),
            pltpu.VMEM((4, group, count), f32),
        ],
        numbers=(me,),
    )
    stats = all_to_all(share, GROUP)
    scratch = [
        whole,
        pltpu.VMEM((group, count, head), bf16),
        pltpu.VMEM((group, head, count), bf16),
        pltpu.VMEM((group, count, head), bf16),
        pltpu.VMEM((length, head), bf16),
        pltpu.VMEM((head, length), bf16),
        pltpu.VMEM((length, head), bf16),
        pltpu.VMEM((length, head), f32),
        pltpu.VMEM((length, head), f32),
    ]
    if not ready:
        scratch.append(pltpu.VMEM((group, head, count), bf16))
    grads = kernel_call(
        functools.partial(backward_kernel, copies, ready, group),
        (piece,) * group,
        (x, *weights, att, dz, stats),
        scratch=scratch,
        numbers=(me,),
    )
    back = exchange(grads)
    outgoing, layer_out = kernel_call(
        functools.partial(finish_kernel, copies, group),
        (((slots, width), bf16), ((count, width), bf16)),
        (*back, mail, slope, gate, mgrad, emb, cot, input_proj, output_proj),
        scratch=[whole],
        numbers=(me,),
    )
    arrived = all_to_all(outgoing.reshape(owners, cap, width), ALL).reshape(slots, width)
    layer_out = moved(layer_out)
    tile = math.gcd(rows_dev, TILE)
    table_grad, layer_out = pl.pallas_call(
        functools.partial(table_kernel, part),
        out_shape=(pltpu.HBM((rows_dev, width), bf16), pltpu.HBM((count, width), bf16)),
        in_specs=[vmem(), vmem(), vmem()],
        out_specs=(hbm(), hbm()),
        scratch_shapes=[
            pltpu.VMEM((rows_dev // tile, tile, width), bf16),
            pltpu.VMEM((2, tile, slots), bf16),
            pltpu.SemaphoreType.DMA((rows_dev // tile + 1,)),
        ],
        compiler_params=params(),
        name="table_grad",
    )(near(wanted), near(arrived), near(layer_out))
    return (layer_out[None], table_grad)


def solution(mesh):
    table, seq = mesh.shape["table"], mesh.shape["seq"]
    if table % 2 or seq % 2 or seq % HEADS or seq & (seq - 1):
        raise ValueError("unsupported mesh")
    finer = Mesh(mesh.devices.reshape(table // 2, 2, 2, seq // 2), ALL)
    placed = (
        P(("a", "b"), ("c", "d")),
        P(("a", "b")),
        P(),
        P(ALL, None),
        P(),
        P(),
        P(("a", "b"), ("c", "d"), None),
    )

    return jax.shard_map(
        local,
        mesh=finer,
        in_specs=placed,
        out_specs=(P(("a", "b"), ("c", "d"), None), P(ALL, None)),
        check_vma=False,
    )
```

```python
import functools
import math

import jax
import jax.numpy as jnp
from jax import lax
from jax.experimental import pallas as pl
from jax.experimental.pallas import tpu as pltpu
from jax.sharding import Mesh, PartitionSpec as P

HEADS = 8
eps_norm = 1e-05
LANES = 128
TILE = 1024
ALL = ("a", "b", "c", "d")
GROUP = ("b", "d")
SWAPPED = ("b", "c")
f32 = jnp.float32
bf16 = jnp.bfloat16
i32 = jnp.int32


def vmem():
    return pl.BlockSpec(memory_space=pltpu.VMEM)


def smem():
    return pl.BlockSpec(memory_space=pltpu.SMEM)


def params():
    return pltpu.CompilerParams(vmem_limit_bytes=24 * 1024 * 1024)


def near(array):
    return pltpu.with_memory_space_constraint(array, pltpu.VMEM)


def far(array):
    return pltpu.with_memory_space_constraint(array, pltpu.HBM)


def hbm():
    return pl.BlockSpec(memory_space=pltpu.HBM)


def kernel_call(kernel, outs, args, scratch=(), numbers=()):
    return pl.pallas_call(
        kernel,
        out_shape=tuple(pltpu.VMEM(shape, dtype) for shape, dtype in outs),
        in_specs=[smem()] * len(numbers) + [vmem()] * len(args),
        out_specs=tuple(vmem() for unused in outs),
        scratch_shapes=list(scratch),
        compiler_params=params(),
    )(*numbers, *map(near, args))


def dot(lhs, rhs, dims=((1,), (0,))):
    return lax.dot_general(lhs, rhs, (dims, ((), ())), preferred_element_type=f32)


def iota(shape, axis):
    return lax.broadcasted_iota(i32, shape, axis)


def to_col(row):
    size = row.shape[1]
    same = iota((size, size), 0) == iota((size, size), 1)
    return jnp.sum(jnp.where(same, row, 0.0), axis=1, keepdims=True)


def to_row(col):
    size = col.shape[0]
    same = iota((size, size), 0) == iota((size, size), 1)
    return jnp.sum(jnp.where(same, col, 0.0), axis=0, keepdims=True)


def request_kernel(
    rows_dev,
    cap,
    unused_s,
    block_s,
    twin_s,
    length_s,
    ids_hbm,
    place_hbm,
    table_hbm,
    mail_ref,
    table_ref,
    ids_s,
    ids_ref,
    place_ref,
    rows_scr,
    sems,
):
    count = ids_ref.shape[1]
    copies = [
        pltpu.make_async_copy(source, target, sems.at[n])
        for n, (source, target) in enumerate(
            [
                (ids_hbm, ids_s),
                (ids_hbm, ids_ref),
                (place_hbm, place_ref),
                (table_hbm, table_ref),
            ]
        )
    ]
    for copy in copies:
        copy.start()
    for copy in copies[:3]:
        copy.wait()

    def fetch(step, unused):
        rows_scr[pl.ds(step, 1), :] = place_ref[pl.ds(ids_s[0, step] >> 7, 1), :]
        return unused

    lax.fori_loop(0, count, fetch, 0, unroll=8)
    lane_col = to_col((ids_ref[...] & (LANES - 1)).astype(f32)).astype(i32)
    lanes = iota((count, LANES), 1)
    stored = jnp.sum(
        jnp.where(lanes == lane_col, rows_scr[...].astype(f32), 0.0), axis=1, keepdims=True
    ).astype(i32)
    shift = rows_dev.bit_length() - 1
    owner = stored >> shift
    local_row = stored & (rows_dev - 1)
    hits = lanes == owner
    hits_f = jnp.where(hits, 1.0, 0.0)
    before = jnp.where(iota((count, count), 1) < iota((count, count), 0), 1.0, 0.0)
    earlier = dot(before.astype(bf16), hits_f.astype(bf16))
    rank = jnp.sum(jnp.where(hits, earlier, 0.0), axis=1, keepdims=True)
    in_rank = lanes == rank.astype(i32)
    asked = local_row + 1
    high = jnp.where(in_rank, (asked >> 7).astype(f32), 0.0).astype(bf16)
    low = jnp.where(in_rank, (asked & 127).astype(f32), 0.0).astype(bf16)
    hits_t = hits_f.T.astype(bf16)
    owners = mail_ref.shape[0]
    wish = dot(hits_t, high) * 128.0 + dot(hits_t, low)
    mail_ref[:, :LANES] = wish[:owners].astype(i32) - 1
    slot = owner.astype(f32) * cap + rank
    live = (block_s[0] * count + iota((1, count), 1)) < length_s[0]
    note = to_row(slot).astype(i32) * 2 + jnp.where(live, 1, 0)
    mail_ref[:, LANES:] = jnp.where(iota((owners, count), 0) == twin_s[0], note, 0)
    copies[3].wait()


def read_note(mail_ref):
    note = jnp.sum(mail_ref[:, LANES:].astype(f32), axis=0, keepdims=True).astype(i32)
    return note >> 1, (note & 1).astype(f32)


def normalize(inputs):
    centred = inputs - jnp.mean(inputs, axis=-1, keepdims=True)
    spread = jnp.sqrt(jnp.mean(centred * centred, axis=-1, keepdims=True) + eps_norm)
    return (centred / spread, spread)


def hand_out(me_s, pieces, source_ref, copies=1):
    for k, piece in enumerate(pieces):
        piece[...] = source_ref[jnp.bitwise_xor(me_s[0], k) // copies]


def take_in(me_s, pieces, target_ref):
    for k, piece in enumerate(pieces):
        target_ref[jnp.bitwise_xor(me_s[0], k)] = piece[...]


def project_kernel(
    copies, me_s, mail_ref, rows_ref, cot_ref, w_ref, wo_ref, emb_ref, slope_ref, gate_ref, mgrad_ref, *refs
):
    pieces, send_ref = refs[:-1], refs[-1]
    slot_row, live_row = read_note(mail_ref)
    count = slot_row.shape[1]
    slots, width = rows_ref.shape
    head = width // HEADS
    slot_col = to_col(slot_row.astype(f32)).astype(i32)
    live_col = to_col(live_row)
    picks = jnp.where(iota((count, slots), 1) == slot_col, 1.0, 0.0).astype(bf16)
    embedded = dot(picks, rows_ref[...])
    emb_ref[...] = embedded.astype(bf16)
    normed, _ = normalize(embedded)
    pre = dot(normed.astype(bf16), w_ref[...])
    cot = jnp.where(live_col > 0.0, cot_ref[...].astype(f32), 0.0).astype(bf16)
    mgrad = dot(cot, wo_ref[...], ((1,), (1,)))
    mgrad_ref[...] = mgrad
    half = 0.5 * pre
    tanh = jnp.tanh(half)
    twice_sig = 1.0 + tanh
    act = half * twice_sig
    slope_ref[...] = 0.5 * (twice_sig + act * (1.0 - tanh))
    gate = act[:, :width]
    gate_ref[...] = gate
    dz = mgrad * gate
    for h in range(HEADS):
        lo = h * head
        send_ref[h] = jnp.concatenate(
            [
                act[:, 2 * width + lo : 2 * width + lo + head],
                act[:, 3 * width + lo : 3 * width + lo + head],
                act[:, width + lo : width + lo + head],
                dz[:, lo : lo + head],
            ],
            axis=1,
        ).astype(bf16)
    hand_out(me_s, pieces, send_ref, copies)


def weight_tile(keys, half_queries_t):
    half = dot(keys, half_queries_t)
    tanh = jnp.tanh(half)
    twice_sig = 1.0 + tanh
    wgt = half * twice_sig
    return wgt, twice_sig + wgt * (1.0 - tanh)


def causal_mask(rows):
    return iota((rows, rows), 0) <= iota((rows, rows), 1)


def forward_kernel(ready, group, me_s, *refs):
    pieces, refs = refs[:group], refs[group:]
    x_ref, att_ref, dz_ref, share_ref, wgt_ref = refs[:5]
    slope_ref = refs[5] if ready else None
    vt_scr, keys_scr, stat_ref = refs[-3:]
    take_in(me_s, pieces, x_ref)
    blocks, rows, cols = x_ref.shape
    head = cols // 4
    scale = head ** (-0.5)
    causal = causal_mask(rows)
    for b in range(blocks):
        span = slice(b * rows, (b + 1) * rows)
        keys_scr[span, :] = x_ref[b, :, head : 2 * head]
        vt_scr[:, span] = x_ref[b, :, 2 * head : 3 * head].astype(f32).T.astype(bf16)
    for b in range(blocks):
        queries_t = (x_ref[b, :, 0:head].astype(f32) * (0.5 * scale)).T.astype(bf16)
        above = b * rows
        upto = above + rows
        wgt, slope = weight_tile(keys_scr[:upto, :], queries_t)
        place = b * (b + 1) // 2 * rows
        if above:
            wgt_ref[place : place + above, :] = wgt[:above].astype(bf16)
        wgt_ref[place + above : place + upto, :] = jnp.where(causal, wgt[above:], 0.0).astype(bf16)
        if ready:
            if above:
                slope_ref[place : place + above, :] = slope[:above]
            slope_ref[place + above : place + upto, :] = jnp.where(causal, slope[above:], 0.0)
        att = dot(vt_scr[:, :upto], wgt_ref[place : place + upto, :])
        dz = x_ref[b, :, 3 * head :].astype(f32).T
        att_ref[b] = att
        dz_ref[b] = dz
        mean = jnp.sum(att, axis=0, keepdims=True) * (1.0 / head)
        cent = att - mean
        share_ref[b, 5 * blocks :, :] = cent.astype(bf16)
        stat_ref[0, b : b + 1, :] = mean
        stat_ref[1, b : b + 1, :] = jnp.sum(cent * cent, axis=0, keepdims=True)
        stat_ref[2, b : b + 1, :] = jnp.sum(dz, axis=0, keepdims=True)
        stat_ref[3, b : b + 1, :] = jnp.sum(cent * dz, axis=0, keepdims=True)
    mean = stat_ref[0]
    high = mean.astype(bf16)
    low = (mean - high.astype(f32)).astype(bf16)
    others = [stat_ref[n].astype(bf16) for n in range(1, 4)]
    for g in range(blocks):
        for n, stat in enumerate([high, low] + others):
            share_ref[g, n * blocks : (n + 1) * blocks, :] = stat


def combine(stats_ref, copies, blocks, head):
    heads = range(0, HEADS * copies, copies)
    width = head * HEADS

    def stat_of(h, n):
        return stats_ref[h, n * blocks : (n + 1) * blocks, :].astype(f32)

    means = [stat_of(h, 0) + stat_of(h, 1) for h in heads]
    mean = sum(means) * (1.0 / HEADS)
    offs = [part - mean for part in means]
    square = 0.0
    dz_sum = 0.0
    dz_att = 0.0
    for h, off in zip(heads, offs):
        square = square + (stat_of(h, 2) + head * (off * off))
        dz_sum = dz_sum + stat_of(h, 3)
        dz_att = dz_att + (stat_of(h, 4) + stat_of(h, 3) * off)
    inv = 1.0 / jnp.sqrt(square * (1.0 / width) + eps_norm)
    return mean, offs, inv, dz_sum * (1.0 / width), dz_att * inv * (1.0 / width)


def output_kernel(
    copies, me_s, share_ref, mail_ref, gate_ref, emb_ref, wo_ref, norm_ref, layer_ref, row_scr
):
    group = share_ref.shape[0]
    width = emb_ref.shape[1]
    head = width // HEADS
    unused, offs, inv, *others = combine(share_ref, copies, group, head)
    for n, rows in enumerate(offs + [inv]):
        row_scr[n] = rows
    mine = pl.ds(me_s[0], 1)
    inv = row_scr[HEADS, mine, :]
    att_t = jnp.concatenate(
        [
            (share_ref[h * copies, 5 * group :, :].astype(f32) + row_scr[h, mine, :]) * inv
            for h in range(HEADS)
        ],
        axis=0,
    )
    att_n = att_t.T
    norm_ref[...] = att_n
    unused, live_row = read_note(mail_ref)
    mixed = (att_n * gate_ref[...]).astype(bf16)
    branch = dot(mixed, wo_ref[...])
    layer_ref[...] = (to_col(live_row) * (emb_ref[...].astype(f32) + branch)).astype(bf16)


def backward_kernel(copies, ready, group, me_s, *refs):
    if ready:
        x_ref, wgt_ref, slope_ref, att_ref, dz_ref, stats_ref = refs[:6]
    else:
        x_ref, wgt_ref, att_ref, dz_ref, stats_ref = refs[:5]
        qt_scr = refs[-1]
    refs = refs[5 + ready :]
    pieces = refs[:group]
    out_ref, da_scr, dat_scr, q_scr, keys_scr, keyst_scr, values_scr, dq_scr, dk_scr, dv_scr = refs[
        group : group + 10
    ]
    blocks, rows, cols = x_ref.shape
    head = cols // 4
    scale = head ** (-0.5)

    def span_of(b):
        return slice(b * rows, (b + 1) * rows)

    mean, _, inv, mean_dz, mean_prod = combine(stats_ref, copies, blocks, head)
    for b in range(blocks):
        att_n = (att_ref[b] - mean[b : b + 1]) * inv[b : b + 1]
        da_t = (dz_ref[b] - mean_dz[b : b + 1] - att_n * mean_prod[b : b + 1]) * inv[b : b + 1]
        dat_scr[b] = (0.5 * da_t).astype(bf16)
        da_scr[b] = da_t.T.astype(bf16)
        q = x_ref[b, :, 0:head].astype(f32) * scale
        q_scr[b] = q.astype(bf16)
        if not ready:
            qt_scr[b] = (0.5 * q).T.astype(bf16)
    causal = causal_mask(rows)
    for b in range(blocks):
        span = slice(b * rows, (b + 1) * rows)
        keys = x_ref[b, :, head : 2 * head]
        keys_scr[span, :] = keys
        keyst_scr[:, span] = keys.astype(f32).T.astype(bf16)
        values_scr[span, :] = x_ref[b, :, 2 * head : 3 * head]
    for b in range(blocks):
        above = b * rows
        upto = above + rows
        place = b * (b + 1) // 2 * rows
        wgt = wgt_ref[place : place + upto, :]
        if ready:
            slope = slope_ref[place : place + upto, :]
        else:
            _, slope = weight_tile(keys_scr[:upto, :], qt_scr[b])
        sgrad = dot(values_scr[:upto, :], dat_scr[b]) * slope
        if not ready:
            mask = iota((upto, rows), 0) <= iota((upto, rows), 1) + above
            sgrad = jnp.where(mask, sgrad, 0.0)
        sgrad = sgrad.astype(bf16)
        dv = dot(wgt, da_scr[b])
        dk = dot(sgrad, q_scr[b])
        if above:
            dv_scr[:above, :] = dv_scr[:above, :] + dv[:above]
            dk_scr[:above, :] = dk_scr[:above, :] + dk[:above]
        dv_scr[above:upto, :] = dv[above:]
        dk_scr[above:upto, :] = dk[above:]
        dq = dot(keyst_scr[:, :upto], sgrad)
        dq_scr[span_of(b), :] = (dq * scale).T
    half = rows // 2
    for b in range(blocks):
        span = span_of(b)
        pair = jnp.concatenate([dq_scr[span, :], dk_scr[span, :]], axis=1)
        out_ref[b, :rows, :] = pair.astype(bf16)
        low = dv_scr[b * rows : b * rows + half, :]
        high = dv_scr[b * rows + half : (b + 1) * rows, :]
        out_ref[b, rows:, :] = jnp.concatenate([low, high], axis=1).astype(bf16)
    hand_out(me_s, pieces, out_ref)


def finish_kernel(copies, group, me_s, *refs):
    pieces, refs = refs[:group], refs[group:]
    mail_ref, slope_ref, norm_ref, mgrad_ref, emb_ref, cot_ref, w_ref, out_ref, grad_ref = refs
    take_in(me_s, pieces, grad_ref)
    slot_row, live_row = read_note(mail_ref)
    count, width = emb_ref.shape
    slots = out_ref.shape[0]
    head = width // HEADS
    live_col = to_col(live_row)
    heads = range(0, HEADS * copies, copies)

    def part(h, span, lanes):
        return grad_ref[h, span, lanes].astype(f32)

    top, low, high = slice(0, count), slice(0, head), slice(head, 2 * head)
    rest = slice(count, count + count // 2)
    queries = jnp.concatenate([part(h, top, low) for h in heads], axis=1)
    keys = jnp.concatenate([part(h, top, high) for h in heads], axis=1)
    values = jnp.concatenate(
        [
            jnp.concatenate([part(h, rest, lanes) for h in heads], axis=1)
            for lanes in (low, high)
        ],
        axis=0,
    )
    act_grad = jnp.concatenate([mgrad_ref[...] * norm_ref[...], values, queries, keys], axis=1)
    pre_grad = (act_grad * slope_ref[...]).astype(bf16)
    norm_grad = dot(pre_grad, w_ref[...], ((1,), (1,)))
    normed, spread = normalize(emb_ref[...].astype(f32))
    mean_grad = jnp.mean(norm_grad, axis=-1, keepdims=True)
    mean_prod = jnp.mean(norm_grad * normed, axis=-1, keepdims=True)
    cot = jnp.where(live_col > 0.0, cot_ref[...].astype(f32), 0.0)
    emb_grad = cot + (norm_grad - mean_grad - normed * mean_prod) / spread
    places = jnp.where(iota((slots, count), 0) == slot_row, 1.0, 0.0).astype(bf16)
    out_ref[...] = dot(places, emb_grad.astype(bf16)).astype(bf16)


def pick_kernel(cap, part, askers, mail_ref, table_ref, out_ref, asked_ref, lane_scr, block_scr):
    rows, width = table_ref.shape
    slots = out_ref.shape[0]
    wish = mail_ref[:, :LANES].astype(f32)
    asked_ref[...] = jnp.concatenate([wish[n : n + 1, :cap] for n in askers], axis=1)
    wish = wish.T
    for taker, asker in enumerate(askers):
        column = jnp.maximum(wish[:cap, asker : asker + 1], 0.0)
        block = jnp.floor(column * (1.0 / part))
        place = slice(taker * cap, (taker + 1) * cap)
        block_scr[place, :] = jnp.broadcast_to(block, (cap, part))
        lane_scr[place, :] = jnp.broadcast_to(column - block * part, (cap, part))
    block = block_scr[...].astype(bf16)
    ramp = iota((slots, part), 1).astype(f32).astype(bf16)
    one = jnp.ones((), bf16)
    zero = jnp.zeros((), bf16)
    lanes = jnp.where(lane_scr[...].astype(bf16) == ramp, one, zero)
    total = jnp.zeros((slots, width), f32)
    for n in range(rows // part):
        picks = jnp.where(block == n, lanes, zero)
        total = total + dot(picks, table_ref[n * part : (n + 1) * part, :])
    out_ref[...] = total.astype(bf16)


def table_kernel(part, asked_ref, arrived_ref, layer_ref, out_hbm, copy_hbm, out_scr, picks_scr, sems):
    chunks, chunk, _ = out_scr.shape
    slots = arrived_ref.shape[0]
    finished = pltpu.make_async_copy(layer_ref, copy_hbm, sems.at[chunks])
    finished.start()
    ramp = iota((part, slots), 0).astype(f32).astype(bf16)
    copies = []
    for n in range(chunks):
        for start in range(0, chunk, part):
            near_row = asked_ref[...] - (n * chunk + start)
            inside = (near_row >= 0) & (near_row < part)
            near_row = jnp.where(inside, near_row, -1.0)
            near_row = jnp.broadcast_to(near_row, (16, slots)).astype(bf16)[0:1]
            picks = jnp.where(ramp == near_row, jnp.ones((), bf16), jnp.zeros((), bf16))
            picks_scr[n % 2, start : start + part, :] = picks
        out_scr[n] = dot(picks_scr[n % 2], arrived_ref[...]).astype(bf16)
        copy = pltpu.make_async_copy(
            out_scr.at[n], out_hbm.at[pl.ds(n * chunk, chunk), :], sems.at[n]
        )
        copy.start()
        copies.append(copy)
    for copy in copies:
        copy.wait()
    finished.wait()


def all_to_all(pieces, axes):
    return lax.all_to_all(pieces, axes, split_axis=0, concat_axis=0, tiled=True)


def local(item_ids, history_len, row_place, item_table, input_proj, output_proj, out_cotangent):
    count = item_ids.shape[1]
    rows_dev, width = item_table.shape
    outer = lax.axis_size("a")
    inner = lax.axis_size("d")
    owners = 4 * outer * inner
    group = 2 * inner
    copies = group // HEADS
    cap = 3 * count // owners
    slots = owners * cap
    head = width // HEADS
    part = math.gcd(rows_dev, 256)
    moved = functools.partial(
        lax.ppermute, axis_name=SWAPPED, perm=[(0, 0), (1, 2), (2, 1), (3, 3)]
    )
    askers = tuple(
        ((a * 2 + c) * 2 + b) * inner + d
        for a in range(outer)
        for b in range(2)
        for c in range(2)
        for d in range(inner)
    )
    at_a, at_b, at_c, at_d = (lax.axis_index(name) for name in ALL)

    def number(value):
        return value.reshape(1).astype(i32)

    me = number(at_b * inner + at_d)

    cot = moved(out_cotangent[0])
    mail, table = pl.pallas_call(
        functools.partial(request_kernel, rows_dev, cap),
        out_shape=(pltpu.VMEM((owners, LANES + count), i32), pltpu.VMEM(item_table.shape, bf16)),
        in_specs=[smem()] * 4 + [hbm()] * 3,
        out_specs=(vmem(), vmem()),
        scratch_shapes=[
            pltpu.SMEM((1, count), i32),
            pltpu.VMEM((1, count), i32),
            pltpu.VMEM((row_place.shape[0] // LANES, LANES), i32),
            pltpu.VMEM((count, LANES), i32),
            pltpu.SemaphoreType.DMA((4,)),
        ],
        compiler_params=params(),
        name="requests",
    )(
        me,
        number(at_c * inner + at_d),
        number(((at_a * 2 + at_c) * 2 + at_b) * inner + at_d),
        history_len,
        far(item_ids),
        far(row_place.reshape(-1, LANES)),
        far(item_table),
    )
    mail = all_to_all(mail, ALL)
    rows, wanted = kernel_call(
        functools.partial(pick_kernel, cap, part, askers),
        (((slots, width), bf16), ((1, slots), f32)),
        (mail, table),
        scratch=[pltpu.VMEM((slots, part), f32), pltpu.VMEM((slots, part), f32)],
    )
    rows = all_to_all(rows.reshape(owners, cap, width), ALL).reshape(slots, width)

    piece = ((count, 4 * head), bf16)
    back_piece = ((count * 3 // 2, 2 * head), bf16)

    def exchange(pieces):
        return [pieces[0]] + [
            lax.ppermute(pieces[k], GROUP, [(g, g ^ k) for g in range(group)])
            for k in range(1, group)
        ]

    emb, slope, gate, mgrad, *sent = kernel_call(
        functools.partial(project_kernel, copies),
        (
            ((count, width), bf16),
            ((count, 4 * width), f32),
            ((count, width), f32),
            ((count, width), f32),
        )
        + (piece,) * group,
        (mail, rows, cot, input_proj, output_proj),
        scratch=[pltpu.VMEM((HEADS, count, 4 * head), bf16)],
        numbers=(me,),
    )
    mine = exchange(sent)
    length = group * count
    tiles = group * (group + 1) // 2 * count
    ready = tiles * count * 6 <= 16 * 1024 * 1024
    x, att, dz, share, *weights = kernel_call(
        functools.partial(forward_kernel, ready, group),
        (
            ((group, count, 4 * head), bf16),
            ((group, head, count), f32),
            ((group, head, count), f32),
            ((group, 5 * group + head, count), bf16),
        )
        + (((tiles, count), bf16),)
        + (((tiles, count), f32),) * ready,
        mine,
        scratch=[
            pltpu.VMEM((head, length), bf16),
            pltpu.VMEM((length, head), bf16),
            pltpu.VMEM((4, group, count), f32),
        ],
        numbers=(me,),
    )
    stats = all_to_all(share, GROUP)
    att_n, layer_out = kernel_call(
        functools.partial(output_kernel, copies),
        (((count, width), f32), ((count, width), bf16)),
        (stats, mail, gate, emb, output_proj),
        scratch=[pltpu.VMEM((HEADS + 1, group, count), f32)],
        numbers=(me,),
    )
    layer_out = moved(layer_out)
    scratch = [
        pltpu.VMEM((group, *back_piece[0]), bf16),
        pltpu.VMEM((group, count, head), bf16),
        pltpu.VMEM((group, head, count), bf16),
        pltpu.VMEM((group, count, head), bf16),
        pltpu.VMEM((length, head), bf16),
        pltpu.VMEM((head, length), bf16),
        pltpu.VMEM((length, head), bf16),
        pltpu.VMEM((length, head), f32),
        pltpu.VMEM((length, head), f32),
        pltpu.VMEM((length, head), f32),
    ]
    if not ready:
        scratch.append(pltpu.VMEM((group, head, count), bf16))
    grads = kernel_call(
        functools.partial(backward_kernel, copies, ready, group),
        (back_piece,) * group,
        (x, *weights, att, dz, stats),
        scratch=scratch,
        numbers=(me,),
    )
    back = exchange(grads)
    (outgoing,) = kernel_call(
        functools.partial(finish_kernel, copies, group),
        (((slots, width), bf16),),
        (*back, mail, slope, att_n, mgrad, emb, cot, input_proj),
        scratch=[pltpu.VMEM((group, *back_piece[0]), bf16)],
        numbers=(me,),
    )
    arrived = all_to_all(outgoing.reshape(owners, cap, width), ALL).reshape(slots, width)
    tile = math.gcd(rows_dev, TILE)
    table_grad, layer_out = pl.pallas_call(
        functools.partial(table_kernel, part),
        out_shape=(pltpu.HBM((rows_dev, width), bf16), pltpu.HBM((count, width), bf16)),
        in_specs=[vmem(), vmem(), vmem()],
        out_specs=(hbm(), hbm()),
        scratch_shapes=[
            pltpu.VMEM((rows_dev // tile, tile, width), bf16),
            pltpu.VMEM((2, tile, slots), bf16),
            pltpu.SemaphoreType.DMA((rows_dev // tile + 1,)),
        ],
        compiler_params=params(),
        name="table_grad",
    )(near(wanted), near(arrived), near(layer_out))
    return (layer_out[None], table_grad)


def solution(mesh):
    table, seq = mesh.shape["table"], mesh.shape["seq"]
    if table % 2 or seq % 2 or seq % HEADS or seq & (seq - 1):
        raise ValueError("unsupported mesh")
    finer = Mesh(mesh.devices.reshape(table // 2, 2, 2, seq // 2), ALL)
    placed = (
        P(("a", "b"), ("c", "d")),
        P(("a", "b")),
        P(),
        P(ALL, None),
        P(),
        P(),
        P(("a", "b"), ("c", "d"), None),
    )

    return jax.shard_map(
        local,
        mesh=finer,
        in_specs=placed,
        out_specs=(P(("a", "b"), ("c", "d"), None), P(ALL, None)),
        check_vma=False,
    )
```

```python
import functools
import math

import jax
import jax.numpy as jnp
from jax import lax
from jax.experimental import pallas as pl
from jax.experimental.pallas import tpu as pltpu
from jax.sharding import Mesh, PartitionSpec as P

HEADS = 8
eps_norm = 1e-05
LANES = 128
TILE = 1024
ALL = ("a", "b", "c", "d")
GROUP = ("b", "d")
SWAPPED = ("b", "c")
f32 = jnp.float32
bf16 = jnp.bfloat16
i32 = jnp.int32


def vmem():
    return pl.BlockSpec(memory_space=pltpu.VMEM)


def smem():
    return pl.BlockSpec(memory_space=pltpu.SMEM)


def params():
    return pltpu.CompilerParams(vmem_limit_bytes=24 * 1024 * 1024)


def near(array):
    return pltpu.with_memory_space_constraint(array, pltpu.VMEM)


def far(array):
    return pltpu.with_memory_space_constraint(array, pltpu.HBM)


def hbm():
    return pl.BlockSpec(memory_space=pltpu.HBM)


def kernel_call(kernel, outs, args, scratch=(), numbers=()):
    return pl.pallas_call(
        kernel,
        out_shape=tuple(pltpu.VMEM(shape, dtype) for shape, dtype in outs),
        in_specs=[smem()] * len(numbers) + [vmem()] * len(args),
        out_specs=tuple(vmem() for unused in outs),
        scratch_shapes=list(scratch),
        compiler_params=params(),
    )(*numbers, *map(near, args))


def dot(lhs, rhs, dims=((1,), (0,))):
    return lax.dot_general(lhs, rhs, (dims, ((), ())), preferred_element_type=f32)


def iota(shape, axis):
    return lax.broadcasted_iota(i32, shape, axis)


def to_col(row):
    size = row.shape[1]
    same = iota((size, size), 0) == iota((size, size), 1)
    return jnp.sum(jnp.where(same, row, 0.0), axis=1, keepdims=True)


def to_row(col):
    size = col.shape[0]
    same = iota((size, size), 0) == iota((size, size), 1)
    return jnp.sum(jnp.where(same, col, 0.0), axis=0, keepdims=True)


def request_kernel(
    rows_dev,
    cap,
    unused_s,
    block_s,
    twin_s,
    length_s,
    ids_hbm,
    place_hbm,
    table_hbm,
    mail_ref,
    table_ref,
    ids_s,
    ids_ref,
    place_ref,
    rows_scr,
    sems,
):
    count = ids_ref.shape[1]
    copies = [
        pltpu.make_async_copy(source, target, sems.at[n])
        for n, (source, target) in enumerate(
            [
                (ids_hbm, ids_s),
                (ids_hbm, ids_ref),
                (place_hbm, place_ref),
                (table_hbm, table_ref),
            ]
        )
    ]
    for copy in copies:
        copy.start()
    for copy in copies[:3]:
        copy.wait()

    def fetch(step, unused):
        rows_scr[pl.ds(step, 1), :] = place_ref[pl.ds(ids_s[0, step] >> 7, 1), :]
        return unused

    lax.fori_loop(0, count, fetch, 0, unroll=8)
    lane_col = to_col((ids_ref[...] & (LANES - 1)).astype(f32)).astype(i32)
    lanes = iota((count, LANES), 1)
    stored = jnp.sum(
        jnp.where(lanes == lane_col, rows_scr[...].astype(f32), 0.0), axis=1, keepdims=True
    ).astype(i32)
    shift = rows_dev.bit_length() - 1
    owner = stored >> shift
    local_row = stored & (rows_dev - 1)
    hits = lanes == owner
    hits_f = jnp.where(hits, 1.0, 0.0)
    before = jnp.where(iota((count, count), 1) < iota((count, count), 0), 1.0, 0.0)
    earlier = dot(before.astype(bf16), hits_f.astype(bf16))
    rank = jnp.sum(jnp.where(hits, earlier, 0.0), axis=1, keepdims=True)
    in_rank = lanes == rank.astype(i32)
    asked = local_row + 1
    high = jnp.where(in_rank, (asked >> 7).astype(f32), 0.0).astype(bf16)
    low = jnp.where(in_rank, (asked & 127).astype(f32), 0.0).astype(bf16)
    hits_t = hits_f.T.astype(bf16)
    owners = mail_ref.shape[0]
    wish = dot(hits_t, high) * 128.0 + dot(hits_t, low)
    mail_ref[:, :LANES] = wish[:owners].astype(i32) - 1
    slot = owner.astype(f32) * cap + rank
    live = (block_s[0] * count + iota((1, count), 1)) < length_s[0]
    note = to_row(slot).astype(i32) * 2 + jnp.where(live, 1, 0)
    mail_ref[:, LANES:] = jnp.where(iota((owners, count), 0) == twin_s[0], note, 0)
    copies[3].wait()


def read_note(mail_ref):
    note = jnp.sum(mail_ref[:, LANES:].astype(f32), axis=0, keepdims=True).astype(i32)
    return note >> 1, (note & 1).astype(f32)


def normalize(inputs):
    centred = inputs - jnp.mean(inputs, axis=-1, keepdims=True)
    spread = jnp.sqrt(jnp.mean(centred * centred, axis=-1, keepdims=True) + eps_norm)
    return (centred / spread, spread)


def hand_out(me_s, pieces, source_ref, copies=1):
    for k, piece in enumerate(pieces):
        piece[...] = source_ref[jnp.bitwise_xor(me_s[0], k) // copies]


def take_in(me_s, pieces, target_ref):
    for k, piece in enumerate(pieces):
        target_ref[jnp.bitwise_xor(me_s[0], k)] = piece[...]


def project_kernel(
    copies, me_s, mail_ref, rows_ref, cot_ref, w_ref, wo_ref, emb_ref, slope_ref, gate_ref, mgrad_ref, *refs
):
    pieces, send_ref = refs[:-1], refs[-1]
    slot_row, live_row = read_note(mail_ref)
    count = slot_row.shape[1]
    slots, width = rows_ref.shape
    head = width // HEADS
    slot_col = to_col(slot_row.astype(f32)).astype(i32)
    live_col = to_col(live_row)
    picks = jnp.where(iota((count, slots), 1) == slot_col, 1.0, 0.0).astype(bf16)
    embedded = dot(picks, rows_ref[...])
    emb_ref[...] = embedded.astype(bf16)
    normed, _ = normalize(embedded)
    pre = dot(normed.astype(bf16), w_ref[...])
    cot = jnp.where(live_col > 0.0, cot_ref[...].astype(f32), 0.0).astype(bf16)
    mgrad = dot(cot, wo_ref[...], ((1,), (1,)))
    mgrad_ref[...] = mgrad
    half = 0.5 * pre
    tanh = jnp.tanh(half)
    twice_sig = 1.0 + tanh
    act = half * twice_sig
    slope_ref[...] = 0.5 * (twice_sig + act * (1.0 - tanh))
    gate = act[:, :width]
    gate_ref[...] = gate
    dz = mgrad * gate
    for h in range(HEADS):
        lo = h * head
        send_ref[h] = jnp.concatenate(
            [
                act[:, 2 * width + lo : 2 * width + lo + head],
                act[:, 3 * width + lo : 3 * width + lo + head],
                act[:, width + lo : width + lo + head],
                dz[:, lo : lo + head],
            ],
            axis=1,
        ).astype(bf16)
    hand_out(me_s, pieces, send_ref, copies)


def weight_tile(keys, half_queries_t):
    half = dot(keys, half_queries_t)
    tanh = jnp.tanh(half)
    twice_sig = 1.0 + tanh
    wgt = half * twice_sig
    return wgt, twice_sig + wgt * (1.0 - tanh)


def causal_mask(rows):
    return iota((rows, rows), 0) <= iota((rows, rows), 1)


def forward_kernel(group, me_s, *refs):
    pieces, refs = refs[:group], refs[group:]
    x_ref, att_ref, dz_ref, wgt_ref = refs[:4]
    shares = refs[4 : 4 + group]
    vt_scr, keys_scr, stat_ref, share_ref = refs[-4:]
    take_in(me_s, pieces, x_ref)
    blocks, rows, cols = x_ref.shape
    head = cols // 4
    scale = head ** (-0.5)
    causal = causal_mask(rows)
    for b in range(blocks):
        span = slice(b * rows, (b + 1) * rows)
        keys_scr[span, :] = x_ref[b, :, head : 2 * head]
        vt_scr[:, span] = x_ref[b, :, 2 * head : 3 * head].astype(f32).T.astype(bf16)
    for b in range(blocks):
        queries_t = (x_ref[b, :, 0:head].astype(f32) * (0.5 * scale)).T.astype(bf16)
        above = b * rows
        upto = above + rows
        wgt, _ = weight_tile(keys_scr[:upto, :], queries_t)
        place = b * (b + 1) // 2 * rows
        if above:
            wgt_ref[place : place + above, :] = wgt[:above].astype(bf16)
        wgt_ref[place + above : place + upto, :] = jnp.where(causal, wgt[above:], 0.0).astype(bf16)
        att = dot(vt_scr[:, :upto], wgt_ref[place : place + upto, :])
        dz = x_ref[b, :, 3 * head :].astype(f32).T
        att_ref[b] = att
        dz_ref[b] = dz
        mean = jnp.sum(att, axis=0, keepdims=True) * (1.0 / head)
        cent = att - mean
        share_ref[b, 5 * blocks :, :] = cent.astype(bf16)
        stat_ref[0, b : b + 1, :] = mean
        stat_ref[1, b : b + 1, :] = jnp.sum(cent * cent, axis=0, keepdims=True)
        stat_ref[2, b : b + 1, :] = jnp.sum(dz, axis=0, keepdims=True)
        stat_ref[3, b : b + 1, :] = jnp.sum(cent * dz, axis=0, keepdims=True)
    mean = stat_ref[0]
    high = mean.astype(bf16)
    low = (mean - high.astype(f32)).astype(bf16)
    others = [stat_ref[n].astype(bf16) for n in range(1, 4)]
    for g in range(blocks):
        for n, stat in enumerate([high, low] + others):
            share_ref[g, n * blocks : (n + 1) * blocks, :] = stat
    hand_out(me_s, shares, share_ref)


def slope_kernel(x_ref, slope_ref, keys_scr):
    blocks, rows, cols = x_ref.shape
    head = cols // 4
    scale = head ** (-0.5)
    causal = causal_mask(rows)
    for b in range(blocks):
        keys_scr[b * rows : (b + 1) * rows, :] = x_ref[b, :, head : 2 * head]
    for b in range(blocks):
        above = b * rows
        upto = above + rows
        place = b * (b + 1) // 2 * rows
        queries_t = (x_ref[b, :, 0:head].astype(f32) * (0.5 * scale)).T.astype(bf16)
        _, slope = weight_tile(keys_scr[:upto, :], queries_t)
        if above:
            slope_ref[place : place + above, :] = slope[:above]
        slope_ref[place + above : place + upto, :] = jnp.where(causal, slope[above:], 0.0)


def combine(stats_ref, copies, blocks, head):
    heads = range(0, HEADS * copies, copies)
    width = head * HEADS

    def stat_of(h, n):
        return stats_ref[h, n * blocks : (n + 1) * blocks, :].astype(f32)

    means = [stat_of(h, 0) + stat_of(h, 1) for h in heads]
    mean = sum(means) * (1.0 / HEADS)
    offs = [part - mean for part in means]
    square = 0.0
    dz_sum = 0.0
    dz_att = 0.0
    for h, off in zip(heads, offs):
        square = square + (stat_of(h, 2) + head * (off * off))
        dz_sum = dz_sum + stat_of(h, 3)
        dz_att = dz_att + (stat_of(h, 4) + stat_of(h, 3) * off)
    inv = 1.0 / jnp.sqrt(square * (1.0 / width) + eps_norm)
    return mean, offs, inv, dz_sum * (1.0 / width), dz_att * inv * (1.0 / width)


def output_kernel(copies, group, me_s, *refs):
    pieces, refs = refs[:group], refs[group:]
    mail_ref, gate_ref, emb_ref, wo_ref, norm_ref, layer_ref, row_scr, share_ref = refs
    take_in(me_s, pieces, share_ref)
    width = emb_ref.shape[1]
    head = width // HEADS
    unused, offs, inv, *others = combine(share_ref, copies, group, head)
    for n, rows in enumerate(offs + [inv]):
        row_scr[n] = rows
    mine = pl.ds(me_s[0], 1)
    inv = row_scr[HEADS, mine, :]
    att_t = jnp.concatenate(
        [
            (share_ref[h * copies, 5 * group :, :].astype(f32) + row_scr[h, mine, :]) * inv
            for h in range(HEADS)
        ],
        axis=0,
    )
    att_n = att_t.T
    norm_ref[...] = att_n
    unused, live_row = read_note(mail_ref)
    mixed = (att_n * gate_ref[...]).astype(bf16)
    branch = dot(mixed, wo_ref[...])
    layer_ref[...] = (to_col(live_row) * (emb_ref[...].astype(f32) + branch)).astype(bf16)


def backward_kernel(copies, ready, group, me_s, *refs):
    shares, refs = refs[:group], refs[group:]
    if ready:
        x_ref, wgt_ref, slope_ref, att_ref, dz_ref = refs[:5]
    else:
        x_ref, wgt_ref, att_ref, dz_ref = refs[:4]
        qt_scr = refs[-1]
    refs = refs[4 + ready :]
    pieces = refs[:group]
    stats_ref, out_ref, da_scr, dat_scr, q_scr = refs[group : group + 5]
    keys_scr, keyst_scr, values_scr, dq_scr, dk_scr, dv_scr = refs[group + 5 : group + 11]
    take_in(me_s, shares, stats_ref)
    blocks, rows, cols = x_ref.shape
    head = cols // 4
    scale = head ** (-0.5)

    def span_of(b):
        return slice(b * rows, (b + 1) * rows)

    mean, _, inv, mean_dz, mean_prod = combine(stats_ref, copies, blocks, head)
    for b in range(blocks):
        att_n = (att_ref[b] - mean[b : b + 1]) * inv[b : b + 1]
        da_t = (dz_ref[b] - mean_dz[b : b + 1] - att_n * mean_prod[b : b + 1]) * inv[b : b + 1]
        dat_scr[b] = (0.5 * da_t).astype(bf16)
        da_scr[b] = da_t.T.astype(bf16)
        q = x_ref[b, :, 0:head].astype(f32) * scale
        q_scr[b] = q.astype(bf16)
        if not ready:
            qt_scr[b] = (0.5 * q).T.astype(bf16)
    causal = causal_mask(rows)
    for b in range(blocks):
        span = slice(b * rows, (b + 1) * rows)
        keys = x_ref[b, :, head : 2 * head]
        keys_scr[span, :] = keys
        keyst_scr[:, span] = keys.astype(f32).T.astype(bf16)
        values_scr[span, :] = x_ref[b, :, 2 * head : 3 * head]
    for b in range(blocks):
        above = b * rows
        upto = above + rows
        place = b * (b + 1) // 2 * rows
        wgt = wgt_ref[place : place + upto, :]
        if ready:
            slope = slope_ref[place : place + upto, :]
        else:
            _, slope = weight_tile(keys_scr[:upto, :], qt_scr[b])
        sgrad = dot(values_scr[:upto, :], dat_scr[b]) * slope
        if not ready:
            mask = iota((upto, rows), 0) <= iota((upto, rows), 1) + above
            sgrad = jnp.where(mask, sgrad, 0.0)
        sgrad = sgrad.astype(bf16)
        dv = dot(wgt, da_scr[b])
        dk = dot(sgrad, q_scr[b])
        if above:
            dv_scr[:above, :] = dv_scr[:above, :] + dv[:above]
            dk_scr[:above, :] = dk_scr[:above, :] + dk[:above]
        dv_scr[above:upto, :] = dv[above:]
        dk_scr[above:upto, :] = dk[above:]
        dq = dot(keyst_scr[:, :upto], sgrad)
        dq_scr[span_of(b), :] = (dq * scale).T
    half = rows // 2
    for b in range(blocks):
        span = span_of(b)
        pair = jnp.concatenate([dq_scr[span, :], dk_scr[span, :]], axis=1)
        out_ref[b, :rows, :] = pair.astype(bf16)
        low = dv_scr[b * rows : b * rows + half, :]
        high = dv_scr[b * rows + half : (b + 1) * rows, :]
        out_ref[b, rows:, :] = jnp.concatenate([low, high], axis=1).astype(bf16)
    hand_out(me_s, pieces, out_ref)


def finish_kernel(copies, group, me_s, *refs):
    pieces, refs = refs[:group], refs[group:]
    mail_ref, slope_ref, norm_ref, mgrad_ref, emb_ref, cot_ref, w_ref, out_ref, grad_ref = refs
    take_in(me_s, pieces, grad_ref)
    slot_row, live_row = read_note(mail_ref)
    count, width = emb_ref.shape
    slots = out_ref.shape[0]
    head = width // HEADS
    live_col = to_col(live_row)
    heads = range(0, HEADS * copies, copies)

    def part(h, span, lanes):
        return grad_ref[h, span, lanes].astype(f32)

    top, low, high = slice(0, count), slice(0, head), slice(head, 2 * head)
    rest = slice(count, count + count // 2)
    queries = jnp.concatenate([part(h, top, low) for h in heads], axis=1)
    keys = jnp.concatenate([part(h, top, high) for h in heads], axis=1)
    values = jnp.concatenate(
        [
            jnp.concatenate([part(h, rest, lanes) for h in heads], axis=1)
            for lanes in (low, high)
        ],
        axis=0,
    )
    act_grad = jnp.concatenate([mgrad_ref[...] * norm_ref[...], values, queries, keys], axis=1)
    pre_grad = (act_grad * slope_ref[...]).astype(bf16)
    norm_grad = dot(pre_grad, w_ref[...], ((1,), (1,)))
    normed, spread = normalize(emb_ref[...].astype(f32))
    mean_grad = jnp.mean(norm_grad, axis=-1, keepdims=True)
    mean_prod = jnp.mean(norm_grad * normed, axis=-1, keepdims=True)
    cot = jnp.where(live_col > 0.0, cot_ref[...].astype(f32), 0.0)
    emb_grad = cot + (norm_grad - mean_grad - normed * mean_prod) / spread
    places = jnp.where(iota((slots, count), 0) == slot_row, 1.0, 0.0).astype(bf16)
    out_ref[...] = dot(places, emb_grad.astype(bf16)).astype(bf16)


def pick_kernel(cap, part, askers, mail_ref, table_ref, out_ref, asked_ref, lane_scr, block_scr):
    rows, width = table_ref.shape
    slots = out_ref.shape[0]
    wish = mail_ref[:, :LANES].astype(f32)
    asked_ref[...] = jnp.concatenate([wish[n : n + 1, :cap] for n in askers], axis=1)
    wish = wish.T
    for taker, asker in enumerate(askers):
        column = jnp.maximum(wish[:cap, asker : asker + 1], 0.0)
        block = jnp.floor(column * (1.0 / part))
        place = slice(taker * cap, (taker + 1) * cap)
        block_scr[place, :] = jnp.broadcast_to(block, (cap, part))
        lane_scr[place, :] = jnp.broadcast_to(column - block * part, (cap, part))
    block = block_scr[...].astype(bf16)
    ramp = iota((slots, part), 1).astype(f32).astype(bf16)
    one = jnp.ones((), bf16)
    zero = jnp.zeros((), bf16)
    lanes = jnp.where(lane_scr[...].astype(bf16) == ramp, one, zero)
    total = jnp.zeros((slots, width), f32)
    for n in range(rows // part):
        picks = jnp.where(block == n, lanes, zero)
        total = total + dot(picks, table_ref[n * part : (n + 1) * part, :])
    out_ref[...] = total.astype(bf16)


def table_kernel(part, asked_ref, arrived_ref, layer_ref, out_hbm, copy_hbm, out_scr, picks_scr, sems):
    chunks, chunk, _ = out_scr.shape
    slots = arrived_ref.shape[0]
    finished = pltpu.make_async_copy(layer_ref, copy_hbm, sems.at[chunks])
    finished.start()
    ramp = iota((part, slots), 0).astype(f32).astype(bf16)
    copies = []
    for n in range(chunks):
        for start in range(0, chunk, part):
            near_row = asked_ref[...] - (n * chunk + start)
            inside = (near_row >= 0) & (near_row < part)
            near_row = jnp.where(inside, near_row, -1.0)
            near_row = jnp.broadcast_to(near_row, (16, slots)).astype(bf16)[0:1]
            picks = jnp.where(ramp == near_row, jnp.ones((), bf16), jnp.zeros((), bf16))
            picks_scr[n % 2, start : start + part, :] = picks
        out_scr[n] = dot(picks_scr[n % 2], arrived_ref[...]).astype(bf16)
        copy = pltpu.make_async_copy(
            out_scr.at[n], out_hbm.at[pl.ds(n * chunk, chunk), :], sems.at[n]
        )
        copy.start()
        copies.append(copy)
    for copy in copies:
        copy.wait()
    finished.wait()


def all_to_all(pieces, axes):
    return lax.all_to_all(pieces, axes, split_axis=0, concat_axis=0, tiled=True)


def local(item_ids, history_len, row_place, item_table, input_proj, output_proj, out_cotangent):
    count = item_ids.shape[1]
    rows_dev, width = item_table.shape
    outer = lax.axis_size("a")
    inner = lax.axis_size("d")
    owners = 4 * outer * inner
    group = 2 * inner
    copies = group // HEADS
    cap = 3 * count // owners
    slots = owners * cap
    head = width // HEADS
    part = math.gcd(rows_dev, 256)
    moved = functools.partial(
        lax.ppermute, axis_name=SWAPPED, perm=[(0, 0), (1, 2), (2, 1), (3, 3)]
    )
    askers = tuple(
        ((a * 2 + c) * 2 + b) * inner + d
        for a in range(outer)
        for b in range(2)
        for c in range(2)
        for d in range(inner)
    )
    at_a, at_b, at_c, at_d = (lax.axis_index(name) for name in ALL)

    def number(value):
        return value.reshape(1).astype(i32)

    me = number(at_b * inner + at_d)

    cot = moved(out_cotangent[0])
    mail, table = pl.pallas_call(
        functools.partial(request_kernel, rows_dev, cap),
        out_shape=(pltpu.VMEM((owners, LANES + count), i32), pltpu.VMEM(item_table.shape, bf16)),
        in_specs=[smem()] * 4 + [hbm()] * 3,
        out_specs=(vmem(), vmem()),
        scratch_shapes=[
            pltpu.SMEM((1, count), i32),
            pltpu.VMEM((1, count), i32),
            pltpu.VMEM((row_place.shape[0] // LANES, LANES), i32),
            pltpu.VMEM((count, LANES), i32),
            pltpu.SemaphoreType.DMA((4,)),
        ],
        compiler_params=params(),
        name="requests",
    )(
        me,
        number(at_c * inner + at_d),
        number(((at_a * 2 + at_c) * 2 + at_b) * inner + at_d),
        history_len,
        far(item_ids),
        far(row_place.reshape(-1, LANES)),
        far(item_table),
    )
    mail = all_to_all(mail, ALL)
    rows, wanted = kernel_call(
        functools.partial(pick_kernel, cap, part, askers),
        (((slots, width), bf16), ((1, slots), f32)),
        (mail, table),
        scratch=[pltpu.VMEM((slots, part), f32), pltpu.VMEM((slots, part), f32)],
    )
    rows = all_to_all(rows.reshape(owners, cap, width), ALL).reshape(slots, width)

    piece = ((count, 4 * head), bf16)
    back_piece = ((count * 3 // 2, 2 * head), bf16)

    def exchange(pieces):
        return [pieces[0]] + [
            lax.ppermute(pieces[k], GROUP, [(g, g ^ k) for g in range(group)])
            for k in range(1, group)
        ]

    emb, slope, gate, mgrad, *sent = kernel_call(
        functools.partial(project_kernel, copies),
        (
            ((count, width), bf16),
            ((count, 4 * width), f32),
            ((count, width), f32),
            ((count, width), f32),
        )
        + (piece,) * group,
        (mail, rows, cot, input_proj, output_proj),
        scratch=[pltpu.VMEM((HEADS, count, 4 * head), bf16)],
        numbers=(me,),
    )
    mine = exchange(sent)
    length = group * count
    tiles = group * (group + 1) // 2 * count
    ready = tiles * count * 6 <= 16 * 1024 * 1024
    share_piece = ((5 * group + head, count), bf16)
    x, att, dz, *weights = kernel_call(
        functools.partial(forward_kernel, group),
        (
            ((group, count, 4 * head), bf16),
            ((group, head, count), f32),
            ((group, head, count), f32),
        )
        + (((tiles, count), bf16),)
        + (share_piece,) * group,
        mine,
        scratch=[
            pltpu.VMEM((head, length), bf16),
            pltpu.VMEM((length, head), bf16),
            pltpu.VMEM((4, group, count), f32),
            pltpu.VMEM((group, *share_piece[0]), bf16),
        ],
        numbers=(me,),
    )
    stats = exchange(weights[-group:])
    weights = weights[:-group]
    if ready:
        weights += kernel_call(
            slope_kernel, (((tiles, count), f32),), (x,), scratch=[pltpu.VMEM((length, head), bf16)]
        )
    att_n, layer_out = kernel_call(
        functools.partial(output_kernel, copies, group),
        (((count, width), f32), ((count, width), bf16)),
        (*stats, mail, gate, emb, output_proj),
        scratch=[
            pltpu.VMEM((HEADS + 1, group, count), f32),
            pltpu.VMEM((group, *share_piece[0]), bf16),
        ],
        numbers=(me,),
    )
    layer_out = moved(layer_out)
    scratch = [
        pltpu.VMEM((group, *share_piece[0]), bf16),
        pltpu.VMEM((group, *back_piece[0]), bf16),
        pltpu.VMEM((group, count, head), bf16),
        pltpu.VMEM((group, head, count), bf16),
        pltpu.VMEM((group, count, head), bf16),
        pltpu.VMEM((length, head), bf16),
        pltpu.VMEM((head, length), bf16),
        pltpu.VMEM((length, head), bf16),
        pltpu.VMEM((length, head), f32),
        pltpu.VMEM((length, head), f32),
        pltpu.VMEM((length, head), f32),
    ]
    if not ready:
        scratch.append(pltpu.VMEM((group, head, count), bf16))
    grads = kernel_call(
        functools.partial(backward_kernel, copies, ready, group),
        (back_piece,) * group,
        (*stats, x, *weights, att, dz),
        scratch=scratch,
        numbers=(me,),
    )
    back = exchange(grads)
    (outgoing,) = kernel_call(
        functools.partial(finish_kernel, copies, group),
        (((slots, width), bf16),),
        (*back, mail, slope, att_n, mgrad, emb, cot, input_proj),
        scratch=[pltpu.VMEM((group, *back_piece[0]), bf16)],
        numbers=(me,),
    )
    arrived = all_to_all(outgoing.reshape(owners, cap, width), ALL).reshape(slots, width)
    tile = math.gcd(rows_dev, TILE)
    table_grad, layer_out = pl.pallas_call(
        functools.partial(table_kernel, part),
        out_shape=(pltpu.HBM((rows_dev, width), bf16), pltpu.HBM((count, width), bf16)),
        in_specs=[vmem(), vmem(), vmem()],
        out_specs=(hbm(), hbm()),
        scratch_shapes=[
            pltpu.VMEM((rows_dev // tile, tile, width), bf16),
            pltpu.VMEM((2, tile, slots), bf16),
            pltpu.SemaphoreType.DMA((rows_dev // tile + 1,)),
        ],
        compiler_params=params(),
        name="table_grad",
    )(near(wanted), near(arrived), near(layer_out))
    return (layer_out[None], table_grad)


def solution(mesh):
    table, seq = mesh.shape["table"], mesh.shape["seq"]
    if table % 2 or seq % 2 or seq % HEADS or seq & (seq - 1):
        raise ValueError("unsupported mesh")
    finer = Mesh(mesh.devices.reshape(table // 2, 2, 2, seq // 2), ALL)
    placed = (
        P(("a", "b"), ("c", "d")),
        P(("a", "b")),
        P(),
        P(ALL, None),
        P(),
        P(),
        P(("a", "b"), ("c", "d"), None),
    )

    return jax.shard_map(
        local,
        mesh=finer,
        in_specs=placed,
        out_specs=(P(("a", "b"), ("c", "d"), None), P(ALL, None)),
        check_vma=False,
    )
```

```python
import functools
import math

import jax
import jax.numpy as jnp
from jax import lax
from jax.experimental import pallas as pl
from jax.experimental.pallas import tpu as pltpu
from jax.sharding import Mesh, PartitionSpec as P

HEADS = 8
eps_norm = 1e-05
LANES = 128
TILE = 1024
ALL = ("a", "b", "c", "d")
GROUP = ("b", "d")
SWAPPED = ("b", "c")
f32 = jnp.float32
bf16 = jnp.bfloat16
i32 = jnp.int32


def vmem():
    return pl.BlockSpec(memory_space=pltpu.VMEM)


def smem():
    return pl.BlockSpec(memory_space=pltpu.SMEM)


def params():
    return pltpu.CompilerParams(vmem_limit_bytes=24 * 1024 * 1024)


def near(array):
    return pltpu.with_memory_space_constraint(array, pltpu.VMEM)


def far(array):
    return pltpu.with_memory_space_constraint(array, pltpu.HBM)


def hbm():
    return pl.BlockSpec(memory_space=pltpu.HBM)


def kernel_call(kernel, outs, args, scratch=(), numbers=()):
    return pl.pallas_call(
        kernel,
        out_shape=tuple(pltpu.VMEM(shape, dtype) for shape, dtype in outs),
        in_specs=[smem()] * len(numbers) + [vmem()] * len(args),
        out_specs=tuple(vmem() for unused in outs),
        scratch_shapes=list(scratch),
        compiler_params=params(),
    )(*numbers, *map(near, args))


def dot(lhs, rhs, dims=((1,), (0,))):
    return lax.dot_general(lhs, rhs, (dims, ((), ())), preferred_element_type=f32)


def iota(shape, axis):
    return lax.broadcasted_iota(i32, shape, axis)


def to_col(row):
    size = row.shape[1]
    same = iota((size, size), 0) == iota((size, size), 1)
    return jnp.sum(jnp.where(same, row, 0.0), axis=1, keepdims=True)


def to_row(col):
    size = col.shape[0]
    same = iota((size, size), 0) == iota((size, size), 1)
    return jnp.sum(jnp.where(same, col, 0.0), axis=0, keepdims=True)


def request_kernel(
    rows_dev,
    cap,
    unused_s,
    block_s,
    twin_s,
    length_s,
    ids_hbm,
    place_hbm,
    table_hbm,
    mail_ref,
    table_ref,
    ids_s,
    ids_ref,
    place_ref,
    rows_scr,
    sems,
):
    count = ids_ref.shape[1]
    copies = [
        pltpu.make_async_copy(source, target, sems.at[n])
        for n, (source, target) in enumerate(
            [
                (ids_hbm, ids_s),
                (ids_hbm, ids_ref),
                (place_hbm, place_ref),
                (table_hbm, table_ref),
            ]
        )
    ]
    for copy in copies:
        copy.start()
    for copy in copies[:3]:
        copy.wait()

    def fetch(step, unused):
        rows_scr[pl.ds(step, 1), :] = place_ref[pl.ds(ids_s[0, step] >> 7, 1), :]
        return unused

    lax.fori_loop(0, count, fetch, 0, unroll=8)
    lane_col = to_col((ids_ref[...] & (LANES - 1)).astype(f32)).astype(i32)
    lanes = iota((count, LANES), 1)
    stored = jnp.sum(
        jnp.where(lanes == lane_col, rows_scr[...].astype(f32), 0.0), axis=1, keepdims=True
    ).astype(i32)
    shift = rows_dev.bit_length() - 1
    owner = stored >> shift
    local_row = stored & (rows_dev - 1)
    hits = lanes == owner
    hits_f = jnp.where(hits, 1.0, 0.0)
    before = jnp.where(iota((count, count), 1) < iota((count, count), 0), 1.0, 0.0)
    earlier = dot(before.astype(bf16), hits_f.astype(bf16))
    rank = jnp.sum(jnp.where(hits, earlier, 0.0), axis=1, keepdims=True)
    in_rank = lanes == rank.astype(i32)
    asked = local_row + 1
    high = jnp.where(in_rank, (asked >> 7).astype(f32), 0.0).astype(bf16)
    low = jnp.where(in_rank, (asked & 127).astype(f32), 0.0).astype(bf16)
    hits_t = hits_f.T.astype(bf16)
    owners = mail_ref.shape[0]
    wish = dot(hits_t, high) * 128.0 + dot(hits_t, low)
    mail_ref[:, :LANES] = wish[:owners].astype(i32) - 1
    slot = owner.astype(f32) * cap + rank
    live = (block_s[0] * count + iota((1, count), 1)) < length_s[0]
    note = to_row(slot).astype(i32) * 2 + jnp.where(live, 1, 0)
    mail_ref[:, LANES:] = jnp.where(iota((owners, count), 0) == twin_s[0], note, 0)
    copies[3].wait()


def read_note(mail_ref):
    note = jnp.sum(mail_ref[:, LANES:].astype(f32), axis=0, keepdims=True).astype(i32)
    return note >> 1, (note & 1).astype(f32)


def normalize(inputs):
    centred = inputs - jnp.mean(inputs, axis=-1, keepdims=True)
    spread = jnp.sqrt(jnp.mean(centred * centred, axis=-1, keepdims=True) + eps_norm)
    return (centred / spread, spread)


def hand_out(me_s, pieces, source_ref, copies=1):
    for k, piece in enumerate(pieces):
        piece[...] = source_ref[jnp.bitwise_xor(me_s[0], k) // copies]


def take_in(me_s, pieces, target_ref):
    for k, piece in enumerate(pieces):
        target_ref[jnp.bitwise_xor(me_s[0], k)] = piece[...]


def project_kernel(
    copies, me_s, mail_ref, rows_ref, cot_ref, w_ref, wo_ref, emb_ref, slope_ref, gate_ref, mgrad_ref, *refs
):
    pieces, send_ref = refs[:-1], refs[-1]
    slot_row, live_row = read_note(mail_ref)
    count = slot_row.shape[1]
    slots, width = rows_ref.shape
    head = width // HEADS
    slot_col = to_col(slot_row.astype(f32)).astype(i32)
    live_col = to_col(live_row)
    picks = jnp.where(iota((count, slots), 1) == slot_col, 1.0, 0.0).astype(bf16)
    embedded = dot(picks, rows_ref[...])
    emb_ref[...] = embedded.astype(bf16)
    normed, _ = normalize(embedded)
    pre = dot(normed.astype(bf16), w_ref[...])
    cot = jnp.where(live_col > 0.0, cot_ref[...].astype(f32), 0.0).astype(bf16)
    mgrad = dot(cot, wo_ref[...], ((1,), (1,)))
    mgrad_ref[...] = mgrad
    half = 0.5 * pre
    tanh = jnp.tanh(half)
    twice_sig = 1.0 + tanh
    act = half * twice_sig
    slope_ref[...] = 0.5 * (twice_sig + act * (1.0 - tanh))
    gate = act[:, :width]
    gate_ref[...] = gate
    dz = mgrad * gate
    for h in range(HEADS):
        lo = h * head
        send_ref[h] = jnp.concatenate(
            [
                act[:, 2 * width + lo : 2 * width + lo + head],
                act[:, 3 * width + lo : 3 * width + lo + head],
                act[:, width + lo : width + lo + head],
                dz[:, lo : lo + head],
            ],
            axis=1,
        ).astype(bf16)
    hand_out(me_s, pieces, send_ref, copies)


def weight_tile(keys, half_queries_t):
    half = dot(keys, half_queries_t)
    tanh = jnp.tanh(half)
    twice_sig = 1.0 + tanh
    wgt = half * twice_sig
    return wgt, twice_sig + wgt * (1.0 - tanh)


def causal_mask(rows):
    return iota((rows, rows), 0) <= iota((rows, rows), 1)


def forward_kernel(group, me_s, *refs):
    pieces, refs = refs[:group], refs[group:]
    x_ref, att_ref, dz_ref, wgt_ref = refs[:4]
    shares = refs[4 : 4 + group]
    vt_scr, keys_scr, stat_ref, share_ref = refs[-4:]
    take_in(me_s, pieces, x_ref)
    blocks, rows, cols = x_ref.shape
    head = cols // 4
    scale = head ** (-0.5)
    causal = causal_mask(rows)
    for b in range(blocks):
        span = slice(b * rows, (b + 1) * rows)
        keys_scr[span, :] = x_ref[b, :, head : 2 * head]
        vt_scr[:, span] = x_ref[b, :, 2 * head : 3 * head].astype(f32).T.astype(bf16)
    for b in range(blocks):
        queries_t = (x_ref[b, :, 0:head].astype(f32) * (0.5 * scale)).T.astype(bf16)
        above = b * rows
        upto = above + rows
        wgt, _ = weight_tile(keys_scr[:upto, :], queries_t)
        place = b * (b + 1) // 2 * rows
        if above:
            wgt_ref[place : place + above, :] = wgt[:above].astype(bf16)
        wgt_ref[place + above : place + upto, :] = jnp.where(causal, wgt[above:], 0.0).astype(bf16)
        att = dot(vt_scr[:, :upto], wgt_ref[place : place + upto, :])
        dz = x_ref[b, :, 3 * head :].astype(f32).T
        att_ref[b] = att
        dz_ref[b] = dz
        mean = jnp.sum(att, axis=0, keepdims=True) * (1.0 / head)
        cent = att - mean
        share_ref[b, 5 * blocks :, :] = cent.astype(bf16)
        stat_ref[0, b : b + 1, :] = mean
        stat_ref[1, b : b + 1, :] = jnp.sum(cent * cent, axis=0, keepdims=True)
        stat_ref[2, b : b + 1, :] = jnp.sum(dz, axis=0, keepdims=True)
        stat_ref[3, b : b + 1, :] = jnp.sum(cent * dz, axis=0, keepdims=True)
    mean = stat_ref[0]
    high = mean.astype(bf16)
    low = (mean - high.astype(f32)).astype(bf16)
    others = [stat_ref[n].astype(bf16) for n in range(1, 4)]
    for g in range(blocks):
        for n, stat in enumerate([high, low] + others):
            share_ref[g, n * blocks : (n + 1) * blocks, :] = stat
    hand_out(me_s, shares, share_ref)


def slope_kernel(x_ref, slope_ref, keys_scr):
    blocks, rows, cols = x_ref.shape
    head = cols // 4
    scale = head ** (-0.5)
    causal = causal_mask(rows)
    for b in range(blocks):
        keys_scr[b * rows : (b + 1) * rows, :] = x_ref[b, :, head : 2 * head]
    for b in range(blocks):
        above = b * rows
        upto = above + rows
        place = b * (b + 1) // 2 * rows
        queries_t = (x_ref[b, :, 0:head].astype(f32) * (0.5 * scale)).T.astype(bf16)
        _, slope = weight_tile(keys_scr[:upto, :], queries_t)
        if above:
            slope_ref[place : place + above, :] = slope[:above]
        slope_ref[place + above : place + upto, :] = jnp.where(causal, slope[above:], 0.0)


def combine(stats_ref, copies, blocks, head):
    heads = range(0, HEADS * copies, copies)
    width = head * HEADS

    def stat_of(h, n):
        return stats_ref[h, n * blocks : (n + 1) * blocks, :].astype(f32)

    means = [stat_of(h, 0) + stat_of(h, 1) for h in heads]
    mean = sum(means) * (1.0 / HEADS)
    offs = [part - mean for part in means]
    square = 0.0
    dz_sum = 0.0
    dz_att = 0.0
    for h, off in zip(heads, offs):
        square = square + (stat_of(h, 2) + head * (off * off))
        dz_sum = dz_sum + stat_of(h, 3)
        dz_att = dz_att + (stat_of(h, 4) + stat_of(h, 3) * off)
    inv = 1.0 / jnp.sqrt(square * (1.0 / width) + eps_norm)
    return mean, offs, inv, dz_sum * (1.0 / width), dz_att * inv * (1.0 / width)


def output_kernel(copies, group, me_s, *refs):
    pieces, refs = refs[:group], refs[group:]
    mail_ref, gate_ref, emb_ref, wo_ref, norm_ref, layer_ref, row_scr, share_ref = refs
    take_in(me_s, pieces, share_ref)
    width = emb_ref.shape[1]
    head = width // HEADS
    unused, offs, inv, *others = combine(share_ref, copies, group, head)
    for n, rows in enumerate(offs + [inv]):
        row_scr[n] = rows
    mine = pl.ds(me_s[0], 1)
    inv = row_scr[HEADS, mine, :]
    att_t = jnp.concatenate(
        [
            (share_ref[h * copies, 5 * group :, :].astype(f32) + row_scr[h, mine, :]) * inv
            for h in range(HEADS)
        ],
        axis=0,
    )
    att_n = att_t.T
    norm_ref[...] = att_n
    unused, live_row = read_note(mail_ref)
    mixed = (att_n * gate_ref[...]).astype(bf16)
    branch = dot(mixed, wo_ref[...])
    layer_ref[...] = (to_col(live_row) * (emb_ref[...].astype(f32) + branch)).astype(bf16)


def backward_kernel(copies, ready, group, me_s, *refs):
    shares, refs = refs[:group], refs[group:]
    if ready:
        x_ref, wgt_ref, slope_ref, att_ref, dz_ref = refs[:5]
    else:
        x_ref, wgt_ref, att_ref, dz_ref = refs[:4]
        qt_scr = refs[-1]
    refs = refs[4 + ready :]
    pieces = refs[:group]
    stats_ref, out_ref, da_scr, dat_scr, q_scr = refs[group : group + 5]
    keys_scr, keyst_scr, values_scr, dq_scr, dk_scr, dv_scr = refs[group + 5 : group + 11]
    take_in(me_s, shares, stats_ref)
    blocks, rows, cols = x_ref.shape
    head = cols // 4
    scale = head ** (-0.5)

    def span_of(b):
        return slice(b * rows, (b + 1) * rows)

    mean, _, inv, mean_dz, mean_prod = combine(stats_ref, copies, blocks, head)
    for b in range(blocks):
        att_n = (att_ref[b] - mean[b : b + 1]) * inv[b : b + 1]
        da_t = (dz_ref[b] - mean_dz[b : b + 1] - att_n * mean_prod[b : b + 1]) * inv[b : b + 1]
        dat_scr[b] = (0.5 * da_t).astype(bf16)
        da_scr[b] = da_t.T.astype(bf16)
        q = x_ref[b, :, 0:head].astype(f32) * scale
        q_scr[b] = q.astype(bf16)
        if not ready:
            qt_scr[b] = (0.5 * q).T.astype(bf16)
    causal = causal_mask(rows)
    for b in range(blocks):
        span = slice(b * rows, (b + 1) * rows)
        keys = x_ref[b, :, head : 2 * head]
        keys_scr[span, :] = keys
        keyst_scr[:, span] = keys.astype(f32).T.astype(bf16)
        values_scr[span, :] = x_ref[b, :, 2 * head : 3 * head]
    for b in range(blocks):
        above = b * rows
        upto = above + rows
        place = b * (b + 1) // 2 * rows
        wgt = wgt_ref[place : place + upto, :]
        if ready:
            slope = slope_ref[place : place + upto, :]
        else:
            _, slope = weight_tile(keys_scr[:upto, :], qt_scr[b])
        sgrad = dot(values_scr[:upto, :], dat_scr[b]) * slope
        if not ready:
            mask = iota((upto, rows), 0) <= iota((upto, rows), 1) + above
            sgrad = jnp.where(mask, sgrad, 0.0)
        sgrad = sgrad.astype(bf16)
        dv = dot(wgt, da_scr[b])
        dk = dot(sgrad, q_scr[b])
        if above:
            dv_scr[:above, :] = dv_scr[:above, :] + dv[:above]
            dk_scr[:above, :] = dk_scr[:above, :] + dk[:above]
        dv_scr[above:upto, :] = dv[above:]
        dk_scr[above:upto, :] = dk[above:]
        dq = dot(keyst_scr[:, :upto], sgrad)
        dq_scr[span_of(b), :] = (dq * scale).T
    half = rows // 2
    for b in range(blocks):
        span = span_of(b)
        pair = jnp.concatenate([dq_scr[span, :], dk_scr[span, :]], axis=1)
        out_ref[b, :rows, :] = pair.astype(bf16)
        low = dv_scr[b * rows : b * rows + half, :]
        high = dv_scr[b * rows + half : (b + 1) * rows, :]
        out_ref[b, rows:, :] = jnp.concatenate([low, high], axis=1).astype(bf16)
    hand_out(me_s, pieces, out_ref)


def prepare_kernel(mail_ref, emb_ref, cot_ref, places_ref, scaled_ref, inv_ref, mask_ref):
    slot_row, live_row = read_note(mail_ref)
    slots, count = places_ref.shape
    places_ref[...] = jnp.where(iota((slots, count), 0) == slot_row, 1.0, 0.0).astype(bf16)
    normed, spread = normalize(emb_ref[...].astype(f32))
    scaled_ref[...] = normed
    inv_ref[...] = jnp.broadcast_to(1.0 / spread, inv_ref.shape)
    mask_ref[...] = jnp.where(to_col(live_row) > 0.0, cot_ref[...].astype(f32), 0.0)


def finish_kernel(copies, group, me_s, *refs):
    pieces, refs = refs[:group], refs[group:]
    places_ref, normed_ref, inv_ref, cot_ref, slope_ref, norm_ref, mgrad_ref, w_ref = refs[:8]
    out_ref, grad_ref = refs[8:]
    take_in(me_s, pieces, grad_ref)
    count, width = normed_ref.shape
    head = width // HEADS
    heads = range(0, HEADS * copies, copies)

    def part(h, span, lanes):
        return grad_ref[h, span, lanes].astype(f32)

    top, low, high = slice(0, count), slice(0, head), slice(head, 2 * head)
    rest = slice(count, count + count // 2)
    queries = jnp.concatenate([part(h, top, low) for h in heads], axis=1)
    keys = jnp.concatenate([part(h, top, high) for h in heads], axis=1)
    values = jnp.concatenate(
        [
            jnp.concatenate([part(h, rest, lanes) for h in heads], axis=1)
            for lanes in (low, high)
        ],
        axis=0,
    )
    act_grad = jnp.concatenate([mgrad_ref[...] * norm_ref[...], values, queries, keys], axis=1)
    pre_grad = (act_grad * slope_ref[...]).astype(bf16)
    norm_grad = dot(pre_grad, w_ref[...], ((1,), (1,)))
    normed = normed_ref[...]
    mean_grad = jnp.mean(norm_grad, axis=-1, keepdims=True)
    mean_prod = jnp.mean(norm_grad * normed, axis=-1, keepdims=True)
    emb_grad = cot_ref[...] + (norm_grad - mean_grad - normed * mean_prod) * inv_ref[:, 0:1]
    out_ref[...] = dot(places_ref[...], emb_grad.astype(bf16)).astype(bf16)


def pick_kernel(cap, part, askers, mail_ref, table_ref, out_ref, asked_ref, lane_scr, block_scr):
    rows, width = table_ref.shape
    slots = out_ref.shape[0]
    wish = mail_ref[:, :LANES].astype(f32)
    asked_ref[...] = jnp.concatenate([wish[n : n + 1, :cap] for n in askers], axis=1)
    wish = wish.T
    for taker, asker in enumerate(askers):
        column = jnp.maximum(wish[:cap, asker : asker + 1], 0.0)
        block = jnp.floor(column * (1.0 / part))
        place = slice(taker * cap, (taker + 1) * cap)
        block_scr[place, :] = jnp.broadcast_to(block, (cap, part))
        lane_scr[place, :] = jnp.broadcast_to(column - block * part, (cap, part))
    block = block_scr[...].astype(bf16)
    ramp = iota((slots, part), 1).astype(f32).astype(bf16)
    one = jnp.ones((), bf16)
    zero = jnp.zeros((), bf16)
    lanes = jnp.where(lane_scr[...].astype(bf16) == ramp, one, zero)
    total = jnp.zeros((slots, width), f32)
    for n in range(rows // part):
        picks = jnp.where(block == n, lanes, zero)
        total = total + dot(picks, table_ref[n * part : (n + 1) * part, :])
    out_ref[...] = total.astype(bf16)


def table_kernel(part, asked_ref, arrived_ref, layer_ref, out_hbm, copy_hbm, out_scr, picks_scr, sems):
    chunks, chunk, _ = out_scr.shape
    slots = arrived_ref.shape[0]
    finished = pltpu.make_async_copy(layer_ref, copy_hbm, sems.at[chunks])
    finished.start()
    ramp = iota((part, slots), 0).astype(f32).astype(bf16)
    copies = []
    for n in range(chunks):
        for start in range(0, chunk, part):
            near_row = asked_ref[...] - (n * chunk + start)
            inside = (near_row >= 0) & (near_row < part)
            near_row = jnp.where(inside, near_row, -1.0)
            near_row = jnp.broadcast_to(near_row, (16, slots)).astype(bf16)[0:1]
            picks = jnp.where(ramp == near_row, jnp.ones((), bf16), jnp.zeros((), bf16))
            picks_scr[n % 2, start : start + part, :] = picks
        out_scr[n] = dot(picks_scr[n % 2], arrived_ref[...]).astype(bf16)
        copy = pltpu.make_async_copy(
            out_scr.at[n], out_hbm.at[pl.ds(n * chunk, chunk), :], sems.at[n]
        )
        copy.start()
        copies.append(copy)
    for copy in copies:
        copy.wait()
    finished.wait()


def all_to_all(pieces, axes):
    return lax.all_to_all(pieces, axes, split_axis=0, concat_axis=0, tiled=True)


def local(item_ids, history_len, row_place, item_table, input_proj, output_proj, out_cotangent):
    count = item_ids.shape[1]
    rows_dev, width = item_table.shape
    outer = lax.axis_size("a")
    inner = lax.axis_size("d")
    owners = 4 * outer * inner
    group = 2 * inner
    copies = group // HEADS
    cap = 3 * count // owners
    slots = owners * cap
    head = width // HEADS
    part = math.gcd(rows_dev, 256)
    moved = functools.partial(
        lax.ppermute, axis_name=SWAPPED, perm=[(0, 0), (1, 2), (2, 1), (3, 3)]
    )
    askers = tuple(
        ((a * 2 + c) * 2 + b) * inner + d
        for a in range(outer)
        for b in range(2)
        for c in range(2)
        for d in range(inner)
    )
    at_a, at_b, at_c, at_d = (lax.axis_index(name) for name in ALL)

    def number(value):
        return value.reshape(1).astype(i32)

    me = number(at_b * inner + at_d)

    cot = moved(out_cotangent[0])
    mail, table = pl.pallas_call(
        functools.partial(request_kernel, rows_dev, cap),
        out_shape=(pltpu.VMEM((owners, LANES + count), i32), pltpu.VMEM(item_table.shape, bf16)),
        in_specs=[smem()] * 4 + [hbm()] * 3,
        out_specs=(vmem(), vmem()),
        scratch_shapes=[
            pltpu.SMEM((1, count), i32),
            pltpu.VMEM((1, count), i32),
            pltpu.VMEM((row_place.shape[0] // LANES, LANES), i32),
            pltpu.VMEM((count, LANES), i32),
            pltpu.SemaphoreType.DMA((4,)),
        ],
        compiler_params=params(),
        name="requests",
    )(
        me,
        number(at_c * inner + at_d),
        number(((at_a * 2 + at_c) * 2 + at_b) * inner + at_d),
        history_len,
        far(item_ids),
        far(row_place.reshape(-1, LANES)),
        far(item_table),
    )
    mail = all_to_all(mail, ALL)
    rows, wanted = kernel_call(
        functools.partial(pick_kernel, cap, part, askers),
        (((slots, width), bf16), ((1, slots), f32)),
        (mail, table),
        scratch=[pltpu.VMEM((slots, part), f32), pltpu.VMEM((slots, part), f32)],
    )
    rows = all_to_all(rows.reshape(owners, cap, width), ALL).reshape(slots, width)

    piece = ((count, 4 * head), bf16)
    back_piece = ((count * 3 // 2, 2 * head), bf16)

    def exchange(pieces):
        return [pieces[0]] + [
            lax.ppermute(pieces[k], GROUP, [(g, g ^ k) for g in range(group)])
            for k in range(1, group)
        ]

    emb, slope, gate, mgrad, *sent = kernel_call(
        functools.partial(project_kernel, copies),
        (
            ((count, width), bf16),
            ((count, 4 * width), f32),
            ((count, width), f32),
            ((count, width), f32),
        )
        + (piece,) * group,
        (mail, rows, cot, input_proj, output_proj),
        scratch=[pltpu.VMEM((HEADS, count, 4 * head), bf16)],
        numbers=(me,),
    )
    mine = exchange(sent)
    prepared = kernel_call(
        prepare_kernel,
        (
            ((slots, count), bf16),
            ((count, width), f32),
            ((count, LANES), f32),
            ((count, width), f32),
        ),
        (mail, emb, cot),
    )
    length = group * count
    tiles = group * (group + 1) // 2 * count
    ready = tiles * count * 6 <= 16 * 1024 * 1024
    share_piece = ((5 * group + head, count), bf16)
    x, att, dz, *weights = kernel_call(
        functools.partial(forward_kernel, group),
        (
            ((group, count, 4 * head), bf16),
            ((group, head, count), f32),
            ((group, head, count), f32),
        )
        + (((tiles, count), bf16),)
        + (share_piece,) * group,
        mine,
        scratch=[
            pltpu.VMEM((head, length), bf16),
            pltpu.VMEM((length, head), bf16),
            pltpu.VMEM((4, group, count), f32),
            pltpu.VMEM((group, *share_piece[0]), bf16),
        ],
        numbers=(me,),
    )
    stats = exchange(weights[-group:])
    weights = weights[:-group]
    if ready:
        weights += kernel_call(
            slope_kernel, (((tiles, count), f32),), (x,), scratch=[pltpu.VMEM((length, head), bf16)]
        )
    att_n, layer_out = kernel_call(
        functools.partial(output_kernel, copies, group),
        (((count, width), f32), ((count, width), bf16)),
        (*stats, mail, gate, emb, output_proj),
        scratch=[
            pltpu.VMEM((HEADS + 1, group, count), f32),
            pltpu.VMEM((group, *share_piece[0]), bf16),
        ],
        numbers=(me,),
    )
    layer_out = moved(layer_out)
    scratch = [
        pltpu.VMEM((group, *share_piece[0]), bf16),
        pltpu.VMEM((group, *back_piece[0]), bf16),
        pltpu.VMEM((group, count, head), bf16),
        pltpu.VMEM((group, head, count), bf16),
        pltpu.VMEM((group, count, head), bf16),
        pltpu.VMEM((length, head), bf16),
        pltpu.VMEM((head, length), bf16),
        pltpu.VMEM((length, head), bf16),
        pltpu.VMEM((length, head), f32),
        pltpu.VMEM((length, head), f32),
        pltpu.VMEM((length, head), f32),
    ]
    if not ready:
        scratch.append(pltpu.VMEM((group, head, count), bf16))
    grads = kernel_call(
        functools.partial(backward_kernel, copies, ready, group),
        (back_piece,) * group,
        (*stats, x, *weights, att, dz),
        scratch=scratch,
        numbers=(me,),
    )
    back = exchange(grads)
    (outgoing,) = kernel_call(
        functools.partial(finish_kernel, copies, group),
        (((slots, width), bf16),),
        (*back, *prepared, slope, att_n, mgrad, input_proj),
        scratch=[pltpu.VMEM((group, *back_piece[0]), bf16)],
        numbers=(me,),
    )
    arrived = all_to_all(outgoing.reshape(owners, cap, width), ALL).reshape(slots, width)
    tile = math.gcd(rows_dev, TILE)
    table_grad, layer_out = pl.pallas_call(
        functools.partial(table_kernel, part),
        out_shape=(pltpu.HBM((rows_dev, width), bf16), pltpu.HBM((count, width), bf16)),
        in_specs=[vmem(), vmem(), vmem()],
        out_specs=(hbm(), hbm()),
        scratch_shapes=[
            pltpu.VMEM((rows_dev // tile, tile, width), bf16),
            pltpu.VMEM((2, tile, slots), bf16),
            pltpu.SemaphoreType.DMA((rows_dev // tile + 1,)),
        ],
        compiler_params=params(),
        name="table_grad",
    )(near(wanted), near(arrived), near(layer_out))
    return (layer_out[None], table_grad)


def solution(mesh):
    table, seq = mesh.shape["table"], mesh.shape["seq"]
    if table % 2 or seq % 2 or seq % HEADS or seq & (seq - 1):
        raise ValueError("unsupported mesh")
    finer = Mesh(mesh.devices.reshape(table // 2, 2, 2, seq // 2), ALL)
    placed = (
        P(("a", "b"), ("c", "d")),
        P(("a", "b")),
        P(),
        P(ALL, None),
        P(),
        P(),
        P(("a", "b"), ("c", "d"), None),
    )

    return jax.shard_map(
        local,
        mesh=finer,
        in_specs=placed,
        out_specs=(P(("a", "b"), ("c", "d"), None), P(ALL, None)),
        check_vma=False,
    )
```
